32 devices in a mesh: outer: 4 (over y, x), inner: 8 (over z, core).
Axes of the slice: x: 2, y: 2, z: 4, core: 2. Of those that a mesh axis runs over, the one named last changes fastest.
Arguments:
- observations: float32 [64, 1024], P(('outer', 'inner')), may hold values from -6 to 6
- obs_precision: float32 [64, 1024], P(('outer', 'inner')), may hold values from 0.001 to 0.1
- obs_values: float32 [1024, 256], replicated, may hold values from -0.375 to 0.375
- obs_pattern: int32 [16, 4], replicated, may hold values 0 or 1
- mix_values: float32 [256, 256], replicated, may hold values from -6 to 6
- trans_pattern: int32 [4, 4], replicated, may hold values 0 or 1
- decay_rate: float32 [256], replicated, may hold values from 0.00078125 to 0.5
- process_var: float32 [256], replicated, may hold values from 0.001 to 0.05
- prior_mean: float32 [256], replicated, may hold values from -6 to 6
- prior_var: float32 [256], replicated, may hold values from 0.1 to 4
Outputs:
- filtered_mean: float32 [64, 256], P(('outer', 'inner'))
- filtered_cov: float32 [64, 256, 256], P(('outer', 'inner'))
The draws below stay inside these ranges and needn't reach their ends.
All inputs are finite; a program needn't handle non-finite values.
Results may differ from the reference program's by a relative error of at most 0.0003.
Values sent between devices are 32-bit elements; how exact they have to be, the bound alone decides.
No kernel may reach another device: no remote copies, remote signals or barrier semaphores. Data moves between devices by JAX's collectives and lax.ppermute only.
A program may use at most 192 MiB of HBM per device.

```python
import math
import jax
import jax.numpy as jnp
from jax import lax

S = 256
M = 1024
BLOCK = 64
STEPS = 64


def plant(entries, key, smallest, largest):
    index_at = [jax.random.randint(jax.random.fold_in(key, axis), (), 0, length) for axis, length in enumerate(entries.shape)]
    main_axis = entries.shape.index(max(entries.shape))
    beside = index_at[:main_axis] + [(index_at[main_axis] + 1) % entries.shape[main_axis]] + index_at[main_axis + 1:]
    return entries.at[tuple(index_at)].set(smallest).at[tuple(beside)].set(largest)


def block_scale(key, shape, split, low, largest):
    def one(dim, blocks):
        draws = jax.random.uniform(jax.random.fold_in(jax.random.fold_in(key, 6), dim), (blocks,), jnp.float32, low / len(split), largest / len(split))
        return jnp.repeat(jnp.exp(draws), shape[dim] // blocks).reshape((-1,) + (1,) * (len(shape) - dim - 1))

    factor_of = one(*split[0])
    for cut in split[1:]:
        factor_of = factor_of * one(*cut)
    return factor_of


def centred(own_key, extent, scale, limit, cuts=(), kind=jnp.bfloat16):
    gain = block_scale(own_key, extent, cuts, -0.22, 0.18) if cuts else 1.0
    array = jax.random.normal(own_key, extent, jnp.float32) * scale * gain
    return jnp.minimum(jnp.maximum(array, -limit), limit).astype(kind)


def setup_inputs(seed: int = 0) -> dict:
    key_list = jax.random.split(jax.random.key(seed), 11)
    observations = centred(key_list[0], (STEPS, M), 1.0, 6.0, ((0, 32),), jnp.float32)
    obs_precision = jnp.clip(jnp.exp(math.log(0.1) - 4.6051702 * jax.random.uniform(key_list[1], (STEPS, M), jnp.float32) ** block_scale(key_list[1], (STEPS, M), ((0, 32),), -0.2, 0.2)), 0.001, 0.1)
    obs_values = centred(key_list[2], (M, S), S ** -0.5, 0.375, (), jnp.float32)
    obs_pattern = plant((jax.random.randint(key_list[3], (M // BLOCK, S // BLOCK), 0, 2) < 1).astype(jnp.int32), jax.random.fold_in(key_list[3], 1), 0, 1)
    mix_values = centred(key_list[4], (S, S), 1.0, 6.0, (), jnp.float32)
    trans_pattern = plant((jax.random.randint(key_list[5], (S // BLOCK, S // BLOCK), 0, 2) < 1).astype(jnp.int32), jax.random.fold_in(key_list[5], 1), 0, 1)
    decay_rate = jnp.clip(jnp.exp(jax.random.uniform(key_list[6], (S,), jnp.float32, math.log(0.00078125), math.log(0.5))), 0.00078125, 0.5)
    process_var = jnp.clip(jnp.exp(jax.random.uniform(key_list[7], (S,), jnp.float32, math.log(0.001), math.log(0.05))), 0.001, 0.05)
    prior_mean = centred(key_list[8], (S,), 1.0, 6.0, (), jnp.float32)
    prior_var = jnp.clip(jnp.exp(jax.random.uniform(key_list[9], (S,), jnp.float32, math.log(0.1), math.log(4.0))), 0.1, 4.0)
    return {"observations": observations, "obs_precision": obs_precision, "obs_values": obs_values, "obs_pattern": obs_pattern, "mix_values": mix_values, "trans_pattern": trans_pattern, "decay_rate": decay_rate, "process_var": process_var, "prior_mean": prior_mean, "prior_var": prior_var}


PRECISE = lax.Precision.HIGHEST

def matmul(left, right):
    return jnp.dot(left, right, precision=PRECISE)

def tmatmul(left, right):
    return lax.dot_general(left, right, (((0,), (0,)), ((), ())), precision=PRECISE)

def gram_rows(left):
    return lax.dot_general(left, left, (((1,), (1,)), ((), ())), precision=PRECISE)

def lower_solve(factor, target):
    return jax.scipy.linalg.solve_triangular(factor, target, lower=True)

def expand_blocks(pattern, block):
    values = pattern.astype(jnp.float32)
    rows_b, cols_b = values.shape
    wide = jnp.broadcast_to(values[:, None, :, None], (rows_b, block, cols_b, block))
    return wide.reshape(rows_b * block, cols_b * block)

def transition(mix_values, trans_pattern, decay_rate):
    blocks = trans_pattern.shape[0]
    pattern = jnp.maximum(trans_pattern, jnp.eye(blocks, dtype=jnp.int32))
    width = mix_values.shape[0]
    coupling = mix_values * expand_blocks(pattern, BLOCK) * (1.0 - jnp.eye(width, dtype=jnp.float32))
    row_abs = jnp.sum(jnp.abs(coupling), axis=1) + 1e-06
    retain = jnp.exp(-decay_rate)
    return jnp.diag(retain) + (0.95 * (1.0 - retain) / row_abs)[:, None] * coupling

def make_element(row_obs, row_prec, obs_matrix, trans_matrix, proc_prec, start_prec, start_info, is_first):
    weighted = obs_matrix * row_prec[:, None]
    gram = tmatmul(weighted, obs_matrix)
    score_vec = jnp.dot(row_prec * row_obs, obs_matrix, precision=PRECISE)
    base_prec = jnp.where(is_first, start_prec, proc_prec)
    base_info = jnp.where(is_first, start_info, jnp.zeros_like(start_info))
    factor = jnp.linalg.cholesky(gram + jnp.diag(base_prec))
    identity_mat = jnp.eye(gram.shape[0], dtype=jnp.float32)
    cov_elem = jax.scipy.linalg.cho_solve((factor, True), identity_mat)
    mean_elem = jax.scipy.linalg.cho_solve((factor, True), base_info + score_vec)
    keep = jnp.where(is_first, jnp.float32(0.0), jnp.float32(1.0))
    trans_elem = jax.scipy.linalg.cho_solve((factor, True), proc_prec[:, None] * trans_matrix) * keep
    info_elem = jnp.dot(score_vec, trans_elem, precision=PRECISE)
    prec_elem = tmatmul(trans_elem, matmul(gram, trans_matrix))
    return (trans_elem, mean_elem, cov_elem, info_elem, prec_elem)

def advance(mean_prev, cov_prev, element):
    trans_elem, mean_elem, cov_elem, info_elem, prec_elem = element
    identity_mat = jnp.eye(cov_prev.shape[0], dtype=jnp.float32)
    factor = jnp.linalg.cholesky(cov_prev)
    middle = identity_mat + tmatmul(factor, matmul(prec_elem, factor))
    factor_mid = jnp.linalg.cholesky(middle)
    spread = lower_solve(factor_mid, matmul(trans_elem, factor).T).T
    cov_new = gram_rows(spread) + cov_elem
    pulled = lower_solve(factor, mean_prev) + jnp.dot(info_elem, factor, precision=PRECISE)
    mean_new = jnp.dot(spread, lower_solve(factor_mid, pulled), precision=PRECISE) + mean_elem
    return (mean_new, cov_new)

def reference(observations, obs_precision, obs_values, obs_pattern, mix_values, trans_pattern, decay_rate, process_var, prior_mean, prior_var):
    obs_matrix = obs_values * expand_blocks(obs_pattern, BLOCK)
    trans_matrix = transition(mix_values, trans_pattern, decay_rate)
    proc_prec = 1.0 / process_var
    start_prec = 1.0 / prior_var
    start_info = prior_mean * start_prec
    width = obs_values.shape[1]

    def step_fn(carry, inputs):
        mean_run, cov_run = carry
        row_obs, row_prec, position = inputs
        element = make_element(row_obs, row_prec, obs_matrix, trans_matrix, proc_prec, start_prec, start_info, position == 0)
        mean_new, cov_new = advance(mean_run, cov_run, element)
        return ((mean_new, cov_new), (mean_new, cov_new))
    initial = (jnp.zeros((width,), jnp.float32), jnp.eye(width, dtype=jnp.float32))
    positions = jnp.arange(observations.shape[0], dtype=jnp.int32)
    unused, outputs = lax.scan(step_fn, initial, (observations, obs_precision, positions))
    return (outputs[0], outputs[1])
```

```python
import functools
import math

import jax
import jax.numpy as jnp
from jax import lax
from jax.experimental import pallas as pl
from jax.experimental.pallas import tpu as pltpu
from jax.sharding import PartitionSpec as P

BLOCK = 64
TAIL = 16
VMEM_LIMIT = 48 << 20
AXES = ("outer", "inner")
F32 = jnp.float32


def dot(left, right, contract=((1,), (0,)), precision=lax.Precision.HIGH):
    return lax.dot_general(
        left, right, (contract, ((), ())), precision=precision, preferred_element_type=F32
    )


def dot_rt(left, right):
    return dot(left, right, ((1,), (1,)))


def eye_of(width):
    rows = lax.broadcasted_iota(jnp.int32, (width, width), 0)
    cols = lax.broadcasted_iota(jnp.int32, (width, width), 1)
    return jnp.where(rows == cols, 1.0, 0.0).astype(F32)


def tail_row(tail, source, target):
    rows = lax.broadcasted_iota(jnp.int32, tail.shape, 0)
    return jnp.where(rows == target, jnp.broadcast_to(tail[source : source + 1], tail.shape), 0.0)


def invert(size, k_ref, yx_ref, norm):
    width = k_ref.shape[1]
    batch = range(size)
    rho = norm / (2.0 + norm)
    alpha = 2.0 / (2.0 + norm)
    scale = 2.0 / (2.0 - rho * rho)
    ident = eye_of(width)
    for b in batch:
        k = k_ref[b]
        squared = yx_ref[b, :width]
        first = alpha * (ident + k)
        second = (alpha * alpha) * (ident + 2.0 * k + squared)
        yx_ref[b, :width] = scale * (2.0 * first - second)
        yx_ref[b, width:] = (scale * alpha) * (2.0 * ident - first)

    def step(rho):
        scale = 2.0 / (2.0 - rho * rho)
        for b in batch:
            both = yx_ref[b]
            yx_ref[b] = scale * (2.0 * both - dot(both, both[:width]))
        return rho * rho / (2.0 - rho * rho)

    lax.while_loop(lambda r: r > 3e-3, step, rho * rho / (2.0 - rho * rho))
    for b in batch:
        x = yx_ref[b, width:]
        lack = ident - x
        rest = lack - dot(k_ref[b], x)
        yx_ref[b, :width] = lack - dot(x, rest)


def prepare(b, left, right, k_ref, yx_ref, full):
    a1, c1, _, v1 = left
    a2, _, j2, v2 = right
    width = c1.shape[0]
    k = dot(c1, j2)
    k_ref[b] = k
    squared = dot(k, k)
    yx_ref[b, :width] = squared
    h = dot(jnp.concatenate([a2, v2]), c1)
    n = dot(jnp.concatenate([a1.T, v1]), j2) if full else None
    return jnp.sum(squared * squared), h, n


def parts(value):
    width = value.shape[1]
    return value[:width], value[width : 2 * width], value[2 * width : 3 * width], value[3 * width :]


def join(pairs, outs, k_ref, yx_ref, full=True, filtered=None):
    size = len(pairs)
    width = k_ref.shape[1]
    sums, hs, ns = zip(*[prepare(b, *pairs[b], k_ref, yx_ref, full) for b in range(size)])
    norm = jnp.sqrt(jnp.sqrt(functools.reduce(jnp.maximum, sums)))
    invert(size, k_ref, yx_ref, norm)
    for b in range(size):
        (a1, c1, j1, v1), (a2, c2, j2, v2) = pairs[b]
        z = yx_ref[b, :width]
        w = a2 - z - dot(a2, z)
        h = hs[b][:width] + c1
        u = tail_row(v1, 0, 0) + tail_row(hs[b][width:], 1, 0)
        cb = dot_rt(jnp.concatenate([h, u]), w)
        b_tail = cb[width:] + u + tail_row(v2, 0, 0)
        c = cb[:width] + h + c2
        if not full:
            outs[b][:width] = c
            outs[b][width:] = b_tail
            continue
        v = a1 - z - dot(z, a1)
        n = ns[b][:width] + j2
        g = tail_row(v2, 1, 1) - tail_row(ns[b][width:], 0, 1)
        je = dot(jnp.concatenate([n, g]), v)
        j = je[:width] + n + j1
        e_tail = je[width:] + g + tail_row(v1, 1, 1)
        outs[b][:width] = dot(w, a1) + w + a1
        outs[b][width : 2 * width] = c
        outs[b][2 * width : 3 * width] = j
        outs[b][3 * width :] = b_tail + e_tail
        if filtered is not None:
            filtered[:width] = v
            filtered[width : 2 * width] = c1 - dot(z, c1)
            filtered[2 * width : 3 * width] = j
            filtered[3 * width :] = u - dot_rt(u, z) + e_tail


def scratch(size, width):
    return [pltpu.VMEM((size, width, width), F32), pltpu.VMEM((size, 2 * width, width), F32)]


def call(kernel, name, outs, ins, size, width, flops, scalars=0, extra=()):
    smem = pl.BlockSpec(memory_space=pltpu.SMEM)
    vmem = pl.BlockSpec(memory_space=pltpu.VMEM)
    return pl.pallas_call(
        kernel,
        name=name,
        out_shape=[jax.ShapeDtypeStruct(*o) if isinstance(o[0], tuple) else jax.ShapeDtypeStruct(o, F32) for o in outs],
        in_specs=[smem] * scalars + [vmem] * (len(ins) - scalars),
        out_specs=[vmem] * len(outs),
        scratch_shapes=list(extra) + (scratch(size, width) if size else []),
        compiler_params=pltpu.CompilerParams(vmem_limit_bytes=VMEM_LIMIT),
        cost_estimate=pl.CostEstimate(flops=flops, bytes_accessed=4 << 20, transcendentals=0),
    )(*ins)


def block_row(pattern, row, blocks, width):
    lanes = lax.broadcasted_iota(jnp.int32, (1, width), 1) // BLOCK
    out = jnp.zeros((1, width), F32)
    for col in range(blocks):
        out = jnp.where(lanes == col, pattern[row, col].astype(F32), out)
    return out


def prep_kernel(obs_pattern, trans_pattern, values, mix, diags, high, low, turned, trans):
    count, width = values.shape
    for i in range(count // BLOCK):
        rows = pl.ds(i * BLOCK, BLOCK)
        block = values[rows] * block_row(obs_pattern, i, width // BLOCK, width)
        high[rows] = block.astype(jnp.bfloat16)
        low[rows] = (block - high[rows].astype(F32)).astype(jnp.bfloat16)
        turned[:, rows] = block.T
    decay = jnp.broadcast_to(diags[3:4], (8, width)).T[:, :1]
    for i in range(width // BLOCK):
        rows = pl.ds(i * BLOCK, BLOCK)
        row_at = lax.broadcasted_iota(jnp.int32, (BLOCK, width), 0) + i * BLOCK
        lanes = lax.broadcasted_iota(jnp.int32, (BLOCK, width), 1)
        mask = block_row(trans_pattern, i, width // BLOCK, width)
        mask = jnp.where(lanes // BLOCK == i, 1.0, mask)
        coupling = jnp.where(row_at == lanes, 0.0, mix[rows] * mask)
        row_abs = jnp.sum(jnp.abs(coupling), axis=1, keepdims=True) + 1e-06
        retain = jnp.exp(-decay[i * BLOCK : (i + 1) * BLOCK])
        trans[rows] = jnp.where(
            row_at == lanes, retain - 1.0, (0.95 * (1.0 - retain) / row_abs) * coupling
        )


def gram_of(weight, high, low, turned):
    scaled = turned[...] * weight
    top = scaled.astype(jnp.bfloat16)
    rest = (scaled - top.astype(F32)).astype(jnp.bfloat16)
    part = functools.partial(jnp.dot, preferred_element_type=F32)
    return part(top, high[...]) + (part(top, low[...]) + part(rest, high[...]))


def leaf(gram, score, first, trans, diags):
    width = trans.shape[0]
    rows = lax.broadcasted_iota(jnp.int32, (TAIL, width), 0)
    ident = eye_of(width)
    mean = jnp.where(first, diags[2:3], jnp.zeros_like(diags[2:3]))
    var = jnp.where(first, diags[1:2], diags[0:1])
    tail = jnp.where(rows == 0, mean, jnp.where(rows == 1, score, 0.0))
    return jnp.where(first, -ident, trans), ident * var, gram, tail


def own_kernel(flags, rows, high, low, turned, trans, diags, target_a, target_b, total, k_ref, yx_ref):
    width = trans.shape[0]
    rows_v = rows[...]
    scores = dot_rt(rows_v[8:16] * rows_v[:8], turned[...])
    grams = [gram_of(rows_v[8 + i : 9 + i], high, low, turned) for i in range(3)]
    t = trans[...]
    first = flags[0] == 0
    no = jnp.bool_(False)
    left = leaf(grams[0], scores[0:1], first, t, diags[...])
    right = leaf(grams[1], scores[1:2], no, t, diags[...])
    join([(left, right)], [total], k_ref, yx_ref, filtered=target_a)
    tail = leaf(grams[2], scores[2:3], no, t, diags[...])[3]
    zero = jnp.zeros((width, width), F32)
    join([(parts(total[...]), (zero, zero, grams[2], tail))], [target_b], k_ref, yx_ref)


def half_kernel(flags, *refs):
    ins, (high, low, turned, trans, diags, total, keep, send) = refs[:4], refs[4:12]
    rows_ref, elements, quads, ahead, grams, scores, k_ref, yx_ref = refs[12:]
    width = trans.shape[0]
    chip = flags[1]
    core = flags[2]
    for slot in range(4):
        rows_ref[slot] = ins[slot][...]
    t = trans[...]
    for j in range(4):
        rows_v = rows_ref[chip ^ j]
        product = rows_v[8:16] * rows_v[:8]
        scores[8 * j : 8 * j + 8] = dot_rt(product, turned[...])
        for i in range(2):
            grams[2 * j + i] = gram_of(rows_v[8 + i : 9 + i], high, low, turned)
    d = diags[...]
    no = jnp.bool_(False)
    pairs = []
    for j in range(4):
        first = (flags[0] == 0) if j == 0 else no
        left = leaf(grams[2 * j], scores[8 * j : 8 * j + 1], first, t, d)
        right = leaf(grams[2 * j + 1], scores[8 * j + 1 : 8 * j + 2], no, t, d)
        pairs.append((left, right))
    join(pairs, [elements.at[j] for j in range(4)], k_ref, yx_ref)
    join(
        [(parts(elements[2 * i]), parts(elements[2 * i + 1])) for i in range(2)],
        [quads.at[i] for i in range(2)],
        k_ref,
        yx_ref,
    )
    odd = chip & 1
    ahead[0] = jnp.where(odd == 1, quads[0], 0.0)
    join(
        [
            (parts(quads[0]), parts(quads[1])),
            (parts(ahead[0]), parts(elements[2 * odd])),
        ],
        [total, ahead.at[1]],
        k_ref,
        yx_ref,
    )
    keep[...] = ahead[core]
    send[...] = ahead[1 - core]


def gather_halves(flags, mine, other):
    core = flags[2] == 0
    return jnp.concatenate([jnp.where(core, mine, other), jnp.where(core, other, mine)])


def total_kernel(halves, flags, *refs):
    if halves:
        mine, other, own, out, half, k_ref, yx_ref = refs
        recv = gather_halves(flags, mine[...], other[...])
    else:
        recv_ref, own, out, half, k_ref, yx_ref = refs
        recv = recv_ref[...]
    later = flags[0] == 1
    here = own[...]
    left = jnp.where(later, recv, here)
    right = jnp.where(later, here, recv)
    join([(parts(left), parts(right))], [out], k_ref, yx_ref)
    middle = out.shape[0] // 2
    half[...] = jnp.where(flags[2] == 0, out[:middle], out[middle:])


def block_target_kernel(flags, keep, recv, here, there, a, b, out_a, out_b, first, k_ref, yx_ref):
    half = flags[1] >> 1
    core = flags[2]
    before = jnp.where(half == 1, jnp.where(core == 0, here[...], there[...]), 0.0)
    near = jnp.where(core == half, keep[...], recv[...])
    join([(parts(before), parts(near))], [first], k_ref, yx_ref)
    left = parts(first[...])
    join([(left, parts(a[...])), (left, parts(b[...]))], [out_a, out_b], k_ref, yx_ref)


def target_kernel(flags, mine, other, a, b, out_a, out_b, k_ref, yx_ref):
    @pl.when(flags[0] == 1)
    def _():
        left = parts(gather_halves(flags, mine[...], other[...]))
        join([(left, parts(a[...])), (left, parts(b[...]))], [out_a, out_b], k_ref, yx_ref)

    @pl.when(flags[0] == 0)
    def _():
        out_a[...] = a[...]
        out_b[...] = b[...]


def final_kernel(state, a, b, mean, cov, out_a, out_b, k_ref, yx_ref):
    width = k_ref.shape[1]
    left = (None, state[:width], None, state[width:])
    join(
        [(left, parts(a[...])), (left, parts(b[...]))],
        [out_a, out_b],
        k_ref,
        yx_ref,
        full=False,
    )
    for i, out in enumerate((out_a, out_b)):
        cov[i] = out[:width]
        mean[i : i + 1] = out[width : width + 1]


def shards(
    observations,
    obs_precision,
    obs_values,
    obs_pattern,
    mix_values,
    trans_pattern,
    decay_rate,
    process_var,
    prior_mean,
    prior_var,
):
    units, width = obs_values.shape
    element = (3 * width + TAIL, width)
    count = lax.axis_size("outer") * lax.axis_size("inner")
    levels = int(math.log2(count))
    place = lax.axis_index("outer") * lax.axis_size("inner") + lax.axis_index("inner")
    cube = 2 * width**3

    def flags_of(first):
        return jnp.stack([first, (place >> 1) & 3, place & 1])

    last = jnp.concatenate([observations[1:], obs_precision[1:]])
    before = lax.ppermute(last, AXES, [(i, i + 1) for i in range(count - 1)])
    diags = jnp.stack([process_var, prior_var, prior_mean, decay_rate])
    high, low, turned, trans = call(
        prep_kernel,
        "prep",
        [((units, width), jnp.bfloat16), ((units, width), jnp.bfloat16), (width, units), (width, width)],
        [obs_pattern, trans_pattern, obs_values, mix_values, diags],
        0,
        width,
        4 * cube,
        scalars=2,
    )
    model = [high, low, turned, trans, diags]
    pad = jnp.zeros((5, units), F32)
    rows = jnp.concatenate([before[:1], observations, pad, before[1:], obs_precision, pad])

    received = []
    for turn in range(4):
        moves = []
        for i in range(count):
            at = i % 8
            moves.append((i, i - at + 2 * ((at & 3) ^ turn) + (at >> 2)))
        received.append(lax.ppermute(rows, AXES, moves))
    target_a, target_b, _ = call(
        own_kernel,
        "own",
        [element] * 3,
        [place[None], rows, *model],
        1,
        width,
        42 * cube,
        scalars=1,
    )
    received, target_a, target_b = lax.optimization_barrier((received, target_a, target_b))
    flags = flags_of((place >> 3) + (place & 1))
    here, keep, send = call(
        half_kernel,
        "half",
        [element] * 3,
        [flags, *received, *model],
        4,
        width,
        150 * cube,
        scalars=1,
        extra=[
            pltpu.VMEM((4, 16, units), F32),
            pltpu.VMEM((4,) + element, F32),
            pltpu.VMEM((2,) + element, F32),
            pltpu.VMEM((2,) + element, F32),
            pltpu.VMEM((8, width, width), F32),
            pltpu.VMEM((32, width), F32),
        ],
    )
    cores = [(i, i ^ 1) for i in range(count)]
    there = lax.ppermute(here, AXES, cores)
    recv = lax.ppermute(send, AXES, cores)
    flags = flags_of(place & 1)
    total, half = call(
        functools.partial(total_kernel, False),
        "total",
        [element, (element[0] // 2, width)],
        [flags, there, here],
        1,
        width,
        15 * cube,
        scalars=1,
    )
    waiting = None
    for level in range(3, levels):
        step = 1 << level
        swap = [(i, i ^ step) for i in range(count)]
        final = level == levels - 1
        if final:
            state = jnp.concatenate([total[width : 2 * width], total[3 * width :]])
            incoming = lax.ppermute(state, AXES, [(i, i ^ step) for i in range(step)])
        else:
            mine = lax.ppermute(half, AXES, swap)
            other = lax.ppermute(mine, AXES, cores)
            incoming = (mine, other)
        if waiting is None:
            target_a, target_b = call(
                block_target_kernel,
                "block_targets",
                [element] * 2,
                [flags, keep, recv, here, there, target_a, target_b],
                2,
                width,
                45 * cube,
                scalars=1,
                extra=[pltpu.VMEM(element, F32)],
            )
        else:
            target_a, target_b = call(
                target_kernel,
                "targets",
                [element] * 2,
                [flags, *waiting, target_a, target_b],
                2,
                width,
                30 * cube,
                scalars=1,
            )
        incoming, target_a, target_b = lax.optimization_barrier((incoming, target_a, target_b))
        if final:
            mean, cov = call(
                final_kernel,
                "final",
                [(2, width), (2, width, width)],
                [incoming, target_a, target_b],
                0,
                width,
                30 * cube,
                extra=[pltpu.VMEM((width + TAIL, width), F32)] * 2 + scratch(2, width),
            )
            return mean, cov
        flags = flags_of((place >> level) & 1)
        waiting = incoming
        total, half = call(
            functools.partial(total_kernel, True),
            "total",
            [element, (element[0] // 2, width)],
            [flags, *incoming, total],
            1,
            width,
            15 * cube,
            scalars=1,
        )


def solution(mesh):
    split = P(AXES, None)
    in_specs = (split, split) + (P(),) * 8
    out_specs = (split, P(AXES, None, None))
    return jax.shard_map(shards, mesh=mesh, in_specs=in_specs, out_specs=out_specs, check_vma=False)
```

```python
import collections
import functools
import math

import jax
import jax.numpy as jnp
from jax import lax
from jax.experimental import pallas as pl
from jax.experimental.pallas import tpu as pltpu
from jax.sharding import PartitionSpec as P

BLOCK = 64
TAIL = 16
VMEM_LIMIT = 48 << 20
AXES = ("outer", "inner")
F32 = jnp.float32
BF16 = jnp.bfloat16


Part = collections.namedtuple("Part", "a c j v diag", defaults=(None,))


def dot(left, right, contract=((1,), (0,))):
    return lax.dot_general(
        left,
        right,
        (contract, ((), ())),
        precision=lax.Precision.HIGH,
        preferred_element_type=F32,
    )


def dot_rt(left, right):
    return dot(left, right, ((1,), (1,)))


def eye_of(width):
    rows = lax.broadcasted_iota(jnp.int32, (width, width), 0)
    cols = lax.broadcasted_iota(jnp.int32, (width, width), 1)
    return jnp.where(rows == cols, 1.0, 0.0).astype(F32)


def tail_row(tail, source, target):
    rows = lax.broadcasted_iota(jnp.int32, tail.shape, 0)
    return jnp.where(rows == target, jnp.broadcast_to(tail[source : source + 1], tail.shape), 0.0)


def parts(value):
    width = value.shape[1]
    return Part(
        value[:width], value[width : 2 * width], value[2 * width : 3 * width], value[3 * width :]
    )


def invert(size, k_ref, yx_ref, norm):
    width = k_ref.shape[1]
    batch = range(size)
    rho = norm / (2.0 + norm)
    alpha = 2.0 / (2.0 + norm)
    scale = 2.0 / (2.0 - rho * rho)
    ident = eye_of(width)
    for b in batch:
        k = k_ref[b]
        squared = yx_ref[b, :width]
        first = alpha * (ident + k)
        second = (alpha * alpha) * (ident + 2.0 * k + squared)
        yx_ref[b, :width] = scale * (2.0 * first - second)
        yx_ref[b, width:] = (scale * alpha) * (2.0 * ident - first)

    def step(rho):
        scale = 2.0 / (2.0 - rho * rho)
        for b in batch:
            both = yx_ref[b]
            yx_ref[b] = scale * (2.0 * both - dot(both, both[:width]))
        return rho * rho / (2.0 - rho * rho)

    lax.while_loop(lambda r: r > 3e-3, step, rho * rho / (2.0 - rho * rho))
    rests = []
    for b in batch:
        x = yx_ref[b, width:]
        rests.append(ident - x - dot(k_ref[b], x))
    for b in batch:
        x = yx_ref[b, width:]
        yx_ref[b, :width] = ident - x - dot(x, rests[b])


def join(pairs, outs, k_ref, yx_ref, full=True):
    width = k_ref.shape[1]
    batch = range(len(pairs))
    for b in batch:
        left, right = pairs[b]
        k_ref[b] = left.diag[0] * right.j if left.diag else dot(left.c, right.j)
    sums = []
    for b in batch:
        squared = dot(k_ref[b], k_ref[b])
        yx_ref[b, :width] = squared
        sums.append(jnp.sum(squared * squared))
    norm = jnp.sqrt(jnp.sqrt(functools.reduce(jnp.maximum, sums)))
    hus, ngs = [], []
    for b in batch:
        left, right = pairs[b]
        stack = right.v if right.a is None else jnp.concatenate([right.a, right.v])
        h = stack * left.diag[1] if left.diag else dot(stack, left.c)
        u = tail_row(left.v, 0, 0) + tail_row(h[-TAIL:], 1, 0)
        h = left.c if right.a is None else h[:width] + left.c
        hus.append(jnp.concatenate([h, u]))
        if full:
            n = dot(jnp.concatenate([left.a.T, left.v]), right.j)
            g = tail_row(right.v, 1, 1) - tail_row(n[width:], 0, 1)
            ngs.append(jnp.concatenate([n[:width] + right.j, g]))
    invert(len(pairs), k_ref, yx_ref, norm)
    ws, vs = [], []
    for b in batch:
        right = pairs[b][1]
        z = yx_ref[b, :width]
        ws.append(-z if right.a is None else right.a - z - dot(right.a, z))
    if full:
        for b in batch:
            left = pairs[b][0]
            z = yx_ref[b, :width]
            vs.append(left.a - z - dot(z, left.a))
    for b in batch:
        left, right = pairs[b]
        cb = hus[b] + dot_rt(hus[b], ws[b])
        c = cb[:width] if right.c is None else cb[:width] + right.c
        tail = cb[width:] + tail_row(right.v, 0, 0)
        if full:
            je = ngs[b] + dot(ngs[b], vs[b])
            tail = tail + je[width:] + tail_row(left.v, 1, 1)
            if right.a is None:
                outs[b][:width] = vs[b]
            else:
                outs[b][:width] = dot(ws[b], left.a) + ws[b] + left.a
            outs[b][2 * width : 3 * width] = je[:width] + left.j
            outs[b][width : 2 * width] = c
            outs[b][3 * width :] = tail
        else:
            outs[b][:width] = c
            outs[b][width:] = tail


def scratch(size, width):
    return [pltpu.VMEM((size, width, width), F32), pltpu.VMEM((size, 2 * width, width), F32)]


def call(kernel, name, outs, ins, size, width, flops, scalars=0, extra=()):
    smem = pl.BlockSpec(memory_space=pltpu.SMEM)
    vmem = pl.BlockSpec(memory_space=pltpu.VMEM)
    shapes = [o if isinstance(o[0], tuple) else (o, F32) for o in outs]
    return pl.pallas_call(
        kernel,
        name=name,
        out_shape=[jax.ShapeDtypeStruct(*o) for o in shapes],
        in_specs=[smem] * scalars + [vmem] * (len(ins) - scalars),
        out_specs=[vmem] * len(outs),
        scratch_shapes=list(extra) + (scratch(size, width) if size else []),
        compiler_params=pltpu.CompilerParams(vmem_limit_bytes=VMEM_LIMIT),
        cost_estimate=pl.CostEstimate(flops=flops, bytes_accessed=4 << 20, transcendentals=0),
    )(*ins)


def block_row(pattern, row, blocks, width):
    lanes = lax.broadcasted_iota(jnp.int32, (1, width), 1) // BLOCK
    out = jnp.zeros((1, width), F32)
    for col in range(blocks):
        out = jnp.where(lanes == col, pattern[row, col].astype(F32), out)
    return out


def columns(rows):
    width = rows.shape[1]
    return jnp.concatenate([rows, jnp.zeros((8 - rows.shape[0], width), F32)]).T


def gram_of(weight, high, low, turned):
    scaled = turned[...] * weight
    top = scaled.astype(BF16)
    rest = (scaled - top.astype(F32)).astype(BF16)
    part = functools.partial(jnp.dot, preferred_element_type=F32)
    return part(top, high[...]) + (part(top, low[...]) + part(rest, high[...]))


def update_of(gram, score):
    rows = lax.broadcasted_iota(jnp.int32, (TAIL, gram.shape[0]), 0)
    return Part(None, None, gram, jnp.where(rows == 1, score, 0.0))


def step_of(gram, score, trans, var):
    width = gram.shape[0]
    return update_of(gram, score)._replace(
        a=trans, c=eye_of(width) * var[0], diag=(var[1], var[0])
    )


def scores_of(rows, turned):
    product = rows[:2] * rows[2:4]
    return dot_rt(jnp.concatenate([product, jnp.zeros((6, rows.shape[1]), F32)]), turned[...])


def prior_of(diags):
    width = diags.shape[1]
    rows = lax.broadcasted_iota(jnp.int32, (TAIL, width), 0)
    return jnp.concatenate(
        [eye_of(width) * diags[1:2], jnp.where(rows == 0, diags[2:3], 0.0)]
    )


def prep_kernel(obs_pattern, trans_pattern, values, mix, diags, high, low, turned, trans):
    count, width = values.shape
    for i in range(count // BLOCK):
        rows = pl.ds(i * BLOCK, BLOCK)
        block = values[rows] * block_row(obs_pattern, i, width // BLOCK, width)
        high[rows] = block.astype(BF16)
        low[rows] = (block - high[rows].astype(F32)).astype(BF16)
        turned[:, rows] = block.T
    decay = columns(diags[3:4])[:, :1]
    for i in range(width // BLOCK):
        rows = pl.ds(i * BLOCK, BLOCK)
        row_at = lax.broadcasted_iota(jnp.int32, (BLOCK, width), 0) + i * BLOCK
        lanes = lax.broadcasted_iota(jnp.int32, (BLOCK, width), 1)
        mask = block_row(trans_pattern, i, width // BLOCK, width)
        mask = jnp.where(lanes // BLOCK == i, 1.0, mask)
        coupling = jnp.where(row_at == lanes, 0.0, mix[rows] * mask)
        row_abs = jnp.sum(jnp.abs(coupling), axis=1, keepdims=True) + 1e-06
        retain = jnp.exp(-decay[i * BLOCK : (i + 1) * BLOCK])
        trans[rows] = jnp.where(
            row_at == lanes, retain - 1.0, (0.95 * (1.0 - retain) / row_abs) * coupling
        )


def own_kernel(rows, high, low, turned, trans, diags, target_a, target_b, k_ref, yx_ref):
    width = trans.shape[0]
    rows_v = rows[...]
    scores = scores_of(rows_v, turned)
    grams = [gram_of(rows_v[2 + i : 3 + i], high, low, turned) for i in range(2)]
    var = diags[0:1]
    first = update_of(grams[0], scores[0:1])
    target_a[: 2 * width] = jnp.zeros((2 * width, width), F32)
    target_a[2 * width : 3 * width] = first.j
    target_a[3 * width :] = first.v
    left = step_of(grams[0], scores[0:1], trans[...], (var, columns(var)[:, :1]))
    join([(left, update_of(grams[1], scores[1:2]))], [target_b], k_ref, yx_ref)


def half_kernel(flags, *refs):
    ins, (high, low, turned, trans, diags, total, keep, send) = refs[:4], refs[4:12]
    rows_ref, elements, quads, ahead, grams, scores, k_ref, yx_ref = refs[12:]
    width = trans.shape[0]
    chip, core = flags[0], flags[1]
    for slot in range(4):
        rows_ref[slot] = ins[slot][...]
    for j in range(4):
        rows_v = rows_ref[chip ^ j]
        scores[8 * j : 8 * j + 8] = scores_of(rows_v, turned)
        for i in range(2):
            grams[2 * j + i] = gram_of(rows_v[2 + i : 3 + i], high, low, turned)
    var = diags[0:1]
    var = (var, columns(var)[:, :1])
    t = trans[...]
    pairs = []
    for j in range(4):
        pairs.append(
            tuple(
                step_of(grams[2 * j + i], scores[8 * j + i : 8 * j + i + 1], t, var)
                for i in range(2)
            )
        )
    join(pairs, [elements.at[j] for j in range(4)], k_ref, yx_ref)
    join(
        [(parts(elements[2 * i]), parts(elements[2 * i + 1])) for i in range(2)],
        [quads.at[i] for i in range(2)],
        k_ref,
        yx_ref,
    )
    odd = chip & 1
    ahead[0] = jnp.where(odd == 1, quads[0], 0.0)
    join(
        [
            (parts(quads[0]), parts(quads[1])),
            (parts(ahead[0]), parts(elements[2 * odd])),
        ],
        [total, ahead.at[1]],
        k_ref,
        yx_ref,
    )
    keep[...] = ahead[core]
    send[...] = ahead[1 - core]


def start_kernel(flags, here, diags, out, state, k_ref, yx_ref):
    width = k_ref.shape[1]
    lead = (flags[1] == 0) & (flags[2] == 0)

    @pl.when(lead)
    def _():
        prior = prior_of(diags[...])
        left = Part(None, prior[:width], None, prior[width:])
        var = diags[1:2]
        left = left._replace(diag=(columns(var)[:, :1], var))
        join([(left, parts(here[...]))], [state], k_ref, yx_ref, full=False)
        out[:width] = -eye_of(width)
        out[width : 2 * width] = state[:width]
        out[2 * width : 3 * width] = jnp.zeros((width, width), F32)
        out[3 * width :] = state[width:]

    @pl.when(jnp.logical_not(lead))
    def _():
        out[...] = here[...]


def total_kernel(full, flags, recv, own, out, *rest):
    k_ref, yx_ref = rest[-2:]

    @pl.when(flags[1] == 0)
    def _():
        later = flags[3] == 1
        there, here = recv[...], own[...]
        left = parts(jnp.where(later, there, here))
        right = parts(jnp.where(later, here, there))
        join([(left, right)], [out], k_ref, yx_ref, full)

    @pl.when(flags[1] != 0)
    def _():
        out[...] = jnp.zeros_like(out)


def block_ahead_kernel(flags, keep, recv, here, there, ahead, k_ref, yx_ref):
    half, core = flags[0] >> 1, flags[1]
    before = jnp.where(half == 1, jnp.where(core == 0, here[...], there[...]), 0.0)
    near = jnp.where(core == half, keep[...], recv[...])
    join([(parts(before), parts(near))], [ahead], k_ref, yx_ref)


def ahead_kernel(flags, mine, other, ahead, out, k_ref, yx_ref):
    @pl.when(flags[3] == 1)
    def _():
        left = parts(jnp.where(flags[1] == 0, mine[...], other[...]))
        join([(left, parts(ahead[...]))], [out], k_ref, yx_ref)

    @pl.when(flags[3] == 0)
    def _():
        out[...] = ahead[...]


def target_kernel(ahead, a, b, out_a, out_b, k_ref, yx_ref):
    left = parts(ahead[...])
    first = parts(a[...])._replace(a=None, c=None)
    join([(left, first), (left, parts(b[...]))], [out_a, out_b], k_ref, yx_ref)


def final_kernel(flags, mine, other, diags, a, b, mean, cov, out_a, out_b, k_ref, yx_ref):
    width = k_ref.shape[1]
    state = jnp.where(flags[1] == 0, mine[...], other[...])
    state = jnp.where(flags[3] == 0, prior_of(diags[...]), state)
    left = Part(None, state[:width], None, state[width:])
    join(
        [(left, parts(a[...])), (left, parts(b[...]))],
        [out_a, out_b],
        k_ref,
        yx_ref,
        full=False,
    )
    for i, out in enumerate((out_a, out_b)):
        cov[i] = out[:width]
        mean[i : i + 1] = out[width : width + 1]


def shards(
    observations,
    obs_precision,
    obs_values,
    obs_pattern,
    mix_values,
    trans_pattern,
    decay_rate,
    process_var,
    prior_mean,
    prior_var,
):
    units, width = obs_values.shape
    element = (3 * width + TAIL, width)
    state = (width + TAIL, width)
    count = lax.axis_size("outer") * lax.axis_size("inner")
    levels = int(math.log2(count))
    place = lax.axis_index("outer") * lax.axis_size("inner") + lax.axis_index("inner")
    cube = 2 * width**3
    evens = range(0, count, 2)
    across = [(i, i + 1) for i in evens]

    def flags_of(first):
        return jnp.stack([(place >> 1) & 3, place & 1, place >> 3, first])

    rows = jnp.concatenate([observations, obs_precision])
    received = []
    for turn in range(4):
        moves = []
        for i in range(count):
            at = i % 8
            moves.append((i, i - at + 2 * ((at & 3) ^ turn) + (at >> 2)))
        received.append(lax.ppermute(rows, AXES, moves))

    diags = jnp.stack([process_var, prior_var, prior_mean, decay_rate])
    high, low, turned, trans = call(
        prep_kernel,
        "prep",
        [((units, width), BF16), ((units, width), BF16), (width, units), (width, width)],
        [obs_pattern, trans_pattern, obs_values, mix_values, diags],
        0,
        width,
        4 * cube,
        scalars=2,
    )
    model = [high, low, turned, trans, diags]
    received, model = lax.optimization_barrier((received, model))
    flags = flags_of(place & 1)
    here, keep, send = call(
        half_kernel,
        "half",
        [element] * 3,
        [flags, *received, *model],
        4,
        width,
        150 * cube,
        scalars=1,
        extra=[
            pltpu.VMEM((4, 4, units), F32),
            pltpu.VMEM((4,) + element, F32),
            pltpu.VMEM((2,) + element, F32),
            pltpu.VMEM((2,) + element, F32),
            pltpu.VMEM((8, width, width), F32),
            pltpu.VMEM((32, width), F32),
        ],
    )
    cores = [(i, i ^ 1) for i in range(count)]
    there = lax.ppermute(here, AXES, cores)
    (total,) = call(
        start_kernel,
        "start",
        [element],
        [flags, here, diags],
        0,
        width,
        10 * cube,
        scalars=1,
        extra=[pltpu.VMEM(state, F32)] + scratch(1, width),
    )
    there, total = lax.optimization_barrier((there, total))
    send, there = lax.optimization_barrier((send, there))
    recv = lax.ppermute(send, AXES, cores)
    ahead = None
    for level in range(2, levels - 1):
        full = level < levels - 2
        if level == 2:
            incoming = there
        else:
            step = 1 << level
            incoming = mine
        flags = flags_of((place >> level) & 1) if level > 2 else flags
        (total,) = call(
            functools.partial(total_kernel, full),
            "total",
            [element if full else state],
            [flags, incoming, total],
            1,
            width,
            15 * cube,
            scalars=1,
        )
        step = 2 << level
        if full:
            mine = lax.ppermute(total, AXES, [(i, i ^ step) for i in evens])
        else:
            mine = lax.ppermute(total, AXES, [(i, i ^ step) for i in evens if i < step])
        if level == 2:
            target_a, target_b = call(
                own_kernel, "own", [element] * 2, [rows, *model], 1, width, 30 * cube
            )
            (ahead,) = call(
                block_ahead_kernel,
                "block_ahead",
                [element],
                [flags, keep, recv, here, there],
                1,
                width,
                15 * cube,
                scalars=1,
            )
            mine, ahead, target_a, target_b = lax.optimization_barrier(
                (mine, ahead, target_a, target_b)
            )
        else:
            (ahead,) = call(
                ahead_kernel,
                "ahead",
                [element],
                [flags, *held, ahead],
                1,
                width,
                15 * cube,
                scalars=1,
            )
            if full:
                mine, ahead = lax.optimization_barrier((mine, ahead))
        if full:
            held = (mine, lax.ppermute(mine, AXES, across))
    target_a, target_b = call(
        target_kernel,
        "targets",
        [element] * 2,
        [ahead, target_a, target_b],
        2,
        width,
        30 * cube,
    )
    mine, target_a, target_b = lax.optimization_barrier((mine, target_a, target_b))
    other = lax.ppermute(mine, AXES, across)
    return call(
        final_kernel,
        "final",
        [(2, width), (2, width, width)],
        [flags_of(place >> (levels - 1)), mine, other, diags, target_a, target_b],
        0,
        width,
        30 * cube,
        scalars=1,
        extra=[pltpu.VMEM(state, F32)] * 2 + scratch(2, width),
    )


def solution(mesh):
    split = P(AXES, None)
    in_specs = (split, split) + (P(),) * 8
    out_specs = (split, P(AXES, None, None))
    return jax.shard_map(shards, mesh=mesh, in_specs=in_specs, out_specs=out_specs, check_vma=False)
```

```python
import collections
import functools
import math

import jax
import jax.numpy as jnp
from jax import lax
from jax.experimental import pallas as pl
from jax.experimental.pallas import tpu as pltpu
from jax.sharding import PartitionSpec as P

BLOCK = 64
TAIL = 16
VMEM_LIMIT = 48 << 20
AXES = ("outer", "inner")
F32 = jnp.float32
BF16 = jnp.bfloat16


Part = collections.namedtuple("Part", "a c j v diag", defaults=(None,))


def dot(left, right, contract=((1,), (0,))):
    return lax.dot_general(
        left,
        right,
        (contract, ((), ())),
        precision=lax.Precision.HIGH,
        preferred_element_type=F32,
    )


def dot_rt(left, right):
    return dot(left, right, ((1,), (1,)))


def eye_of(width):
    rows = lax.broadcasted_iota(jnp.int32, (width, width), 0)
    cols = lax.broadcasted_iota(jnp.int32, (width, width), 1)
    return jnp.where(rows == cols, 1.0, 0.0).astype(F32)


def tail_row(tail, source, target):
    rows = lax.broadcasted_iota(jnp.int32, tail.shape, 0)
    return jnp.where(rows == target, jnp.broadcast_to(tail[source : source + 1], tail.shape), 0.0)


def parts(value):
    width = value.shape[1]
    return Part(
        value[:width], value[width : 2 * width], value[2 * width : 3 * width], value[3 * width :]
    )


def invert(size, k_ref, yx_ref, norm):
    width = k_ref.shape[1]
    batch = range(size)
    tiny = norm <= 1e-2
    small = jnp.logical_and(norm <= 5e-2, jnp.logical_not(tiny))

    @pl.when(tiny)
    def _():
        for b in batch:
            yx_ref[b, :width] = k_ref[b] - yx_ref[b, :width]

    @pl.when(small)
    def _():
        for b in batch:
            squared = yx_ref[b, :width]
            begun = k_ref[b] - squared
            yx_ref[b, :width] = begun + dot(begun, squared)

    @pl.when(norm > 5e-2)
    def _():
        iterate(size, k_ref, yx_ref, norm)


def iterate(size, k_ref, yx_ref, norm):
    width = k_ref.shape[1]
    batch = range(size)
    rho = norm / (2.0 + norm)
    alpha = 2.0 / (2.0 + norm)
    scale = 2.0 / (2.0 - rho * rho)
    ident = eye_of(width)
    for b in batch:
        k = k_ref[b]
        squared = yx_ref[b, :width]
        first = alpha * (ident + k)
        second = (alpha * alpha) * (ident + 2.0 * k + squared)
        yx_ref[b, :width] = scale * (2.0 * first - second)
        yx_ref[b, width:] = (scale * alpha) * (2.0 * ident - first)

    def step(rho):
        scale = 2.0 / (2.0 - rho * rho)
        for b in batch:
            both = yx_ref[b]
            yx_ref[b] = scale * (2.0 * both - dot(both, both[:width]))
        return rho * rho / (2.0 - rho * rho)

    lax.while_loop(lambda r: r > 3e-3, step, rho * rho / (2.0 - rho * rho))
    rests = []
    for b in batch:
        x = yx_ref[b, width:]
        rests.append(ident - x - dot(k_ref[b], x))
    for b in batch:
        x = yx_ref[b, width:]
        yx_ref[b, :width] = ident - x - dot(x, rests[b])


def join(pairs, outs, k_ref, yx_ref, full=True):
    width = k_ref.shape[1]
    batch = range(len(pairs))
    for b in batch:
        left, right = pairs[b]
        k_ref[b] = left.diag[0] * right.j if left.diag else dot(left.c, right.j)
    sums = []
    for b in batch:
        squared = dot(k_ref[b], k_ref[b])
        yx_ref[b, :width] = squared
        sums.append(jnp.sum(squared * squared))
    norm = jnp.sqrt(jnp.sqrt(functools.reduce(jnp.maximum, sums)))
    hus, ngs = [], []
    for b in batch:
        left, right = pairs[b]
        stack = right.v if right.a is None else jnp.concatenate([right.a, right.v])
        h = stack * left.diag[1] if left.diag else dot(stack, left.c)
        u = tail_row(left.v, 0, 0) + tail_row(h[-TAIL:], 1, 0)
        h = left.c if right.a is None else h[:width] + left.c
        hus.append(jnp.concatenate([h, u]))
        if full:
            n = dot(jnp.concatenate([left.a.T, left.v]), right.j)
            g = tail_row(right.v, 1, 1) - tail_row(n[width:], 0, 1)
            ngs.append(jnp.concatenate([n[:width] + right.j, g]))
    invert(len(pairs), k_ref, yx_ref, norm)
    ws, vs = [], []
    for b in batch:
        right = pairs[b][1]
        z = yx_ref[b, :width]
        ws.append(-z if right.a is None else right.a - z - dot(right.a, z))
    if full:
        for b in batch:
            left = pairs[b][0]
            z = yx_ref[b, :width]
            vs.append(left.a - z - dot(z, left.a))
    for b in batch:
        left, right = pairs[b]
        cb = hus[b] + dot_rt(hus[b], ws[b])
        c = cb[:width] if right.c is None else cb[:width] + right.c
        tail = cb[width:] + tail_row(right.v, 0, 0)
        if full:
            je = ngs[b] + dot(ngs[b], vs[b])
            tail = tail + je[width:] + tail_row(left.v, 1, 1)
            if right.a is None:
                outs[b][:width] = vs[b]
            else:
                outs[b][:width] = dot(ws[b], left.a) + ws[b] + left.a
            outs[b][2 * width : 3 * width] = je[:width] + left.j
            outs[b][width : 2 * width] = c
            outs[b][3 * width :] = tail
        else:
            outs[b][:width] = c
            outs[b][width:] = tail


def scratch(size, width):
    return [pltpu.VMEM((size, width, width), F32), pltpu.VMEM((size, 2 * width, width), F32)]


def call(kernel, name, outs, ins, size, width, flops, scalars=0, extra=(), placed=()):
    smem = pl.BlockSpec(memory_space=pltpu.SMEM)
    vmem = pl.BlockSpec(memory_space=pltpu.VMEM)
    shapes = [o if isinstance(o[0], tuple) else (o, F32) for o in outs]
    return pl.pallas_call(
        kernel,
        name=name,
        out_shape=[jax.ShapeDtypeStruct(*o) for o in shapes],
        in_specs=[
            pl.BlockSpec(memory_space=pl.ANY) if i in placed else smem if i < scalars else vmem
            for i in range(len(ins))
        ],
        out_specs=[vmem] * len(outs),
        scratch_shapes=list(extra) + (scratch(size, width) if size else []),
        compiler_params=pltpu.CompilerParams(vmem_limit_bytes=VMEM_LIMIT),
        cost_estimate=pl.CostEstimate(flops=flops, bytes_accessed=4 << 20, transcendentals=0),
    )(*ins)


def block_row(pattern, row, blocks, width):
    lanes = lax.broadcasted_iota(jnp.int32, (1, width), 1) // BLOCK
    out = jnp.zeros((1, width), F32)
    for col in range(blocks):
        out = jnp.where(lanes == col, pattern[row, col].astype(F32), out)
    return out


def columns(rows):
    width = rows.shape[1]
    return jnp.concatenate([rows, jnp.zeros((8 - rows.shape[0], width), F32)]).T


def gram_of(weight, high, low, turned):
    scaled = turned[...] * weight
    top = scaled.astype(BF16)
    rest = (scaled - top.astype(F32)).astype(BF16)
    part = functools.partial(jnp.dot, preferred_element_type=F32)
    return part(top, high[...]) + (part(top, low[...]) + part(rest, high[...]))


def update_of(gram, score):
    rows = lax.broadcasted_iota(jnp.int32, (TAIL, gram.shape[0]), 0)
    return Part(None, None, gram, jnp.where(rows == 1, score, 0.0))


def step_of(gram, score, trans, var):
    width = gram.shape[0]
    return update_of(gram, score)._replace(
        a=trans, c=eye_of(width) * var[0], diag=(var[1], var[0])
    )


def scores_of(rows, turned):
    product = rows[:2] * rows[2:4]
    return dot_rt(jnp.concatenate([product, jnp.zeros((6, rows.shape[1]), F32)]), turned[...])


def prior_of(diags):
    width = diags.shape[1]
    rows = lax.broadcasted_iota(jnp.int32, (TAIL, width), 0)
    return jnp.concatenate(
        [eye_of(width) * diags[1:2], jnp.where(rows == 0, diags[2:3], 0.0)]
    )


def prep_kernel(
    obs_pattern, trans_pattern, values_at, mix_at, diags, high, low, turned, trans, values, mix, sems
):
    count, width = values.shape
    pieces = 4
    piece = count // pieces
    copies = []
    for i in range(pieces):
        rows = pl.ds(i * piece, piece)
        copies.append(pltpu.make_async_copy(values_at.at[rows], values.at[rows], sems.at[i]))
    copies.append(pltpu.make_async_copy(mix_at, mix, sems.at[pieces]))
    for copy in copies:
        copy.start()
    for i in range(count // BLOCK):
        if i * BLOCK % piece == 0:
            copies[i * BLOCK // piece].wait()
        rows = pl.ds(i * BLOCK, BLOCK)
        block = values[rows] * block_row(obs_pattern, i, width // BLOCK, width)
        high[rows] = block.astype(BF16)
        low[rows] = (block - high[rows].astype(F32)).astype(BF16)
        turned[:, rows] = block.T
    copies[pieces].wait()
    decay = columns(diags[3:4])[:, :1]
    for i in range(width // BLOCK):
        rows = pl.ds(i * BLOCK, BLOCK)
        row_at = lax.broadcasted_iota(jnp.int32, (BLOCK, width), 0) + i * BLOCK
        lanes = lax.broadcasted_iota(jnp.int32, (BLOCK, width), 1)
        mask = block_row(trans_pattern, i, width // BLOCK, width)
        mask = jnp.where(lanes // BLOCK == i, 1.0, mask)
        coupling = jnp.where(row_at == lanes, 0.0, mix[rows] * mask)
        row_abs = jnp.sum(jnp.abs(coupling), axis=1, keepdims=True) + 1e-06
        retain = jnp.exp(-decay[i * BLOCK : (i + 1) * BLOCK])
        trans[rows] = jnp.where(
            row_at == lanes, retain - 1.0, (0.95 * (1.0 - retain) / row_abs) * coupling
        )


def own_kernel(rows, high, low, turned, trans, diags, target_a, target_b, k_ref, yx_ref):
    width = trans.shape[0]
    rows_v = rows[...]
    scores = scores_of(rows_v, turned)
    grams = [gram_of(rows_v[2 + i : 3 + i], high, low, turned) for i in range(2)]
    var = diags[0:1]
    first = update_of(grams[0], scores[0:1])
    target_a[: 2 * width] = jnp.zeros((2 * width, width), F32)
    target_a[2 * width : 3 * width] = first.j
    target_a[3 * width :] = first.v
    left = step_of(grams[0], scores[0:1], trans[...], (var, columns(var)[:, :1]))
    join([(left, update_of(grams[1], scores[1:2]))], [target_b], k_ref, yx_ref)


def half_kernel(flags, *refs):
    ins, (high, low, turned, trans, diags, total, keep, send) = refs[:4], refs[4:12]
    rows_ref, elements, quads, ahead, grams, scores, k_ref, yx_ref = refs[12:]
    width = trans.shape[0]
    chip, core = flags[0], flags[1]
    for slot in range(4):
        rows_ref[slot] = ins[slot][...]
    for j in range(4):
        rows_v = rows_ref[chip ^ j]
        scores[8 * j : 8 * j + 8] = scores_of(rows_v, turned)
        for i in range(2):
            grams[2 * j + i] = gram_of(rows_v[2 + i : 3 + i], high, low, turned)
    var = diags[0:1]
    var = (var, columns(var)[:, :1])
    t = trans[...]
    pairs = []
    for j in range(4):
        pairs.append(
            tuple(
                step_of(grams[2 * j + i], scores[8 * j + i : 8 * j + i + 1], t, var)
                for i in range(2)
            )
        )
    join(pairs, [elements.at[j] for j in range(4)], k_ref, yx_ref)
    join(
        [(parts(elements[2 * i]), parts(elements[2 * i + 1])) for i in range(2)],
        [quads.at[i] for i in range(2)],
        k_ref,
        yx_ref,
    )
    odd = chip & 1
    ahead[0] = jnp.where(odd == 1, quads[0], 0.0)
    join(
        [
            (parts(quads[0]), parts(quads[1])),
            (parts(ahead[0]), parts(elements[2 * odd])),
        ],
        [total, ahead.at[1]],
        k_ref,
        yx_ref,
    )
    keep[...] = ahead[core]
    send[...] = ahead[1 - core]


def start_kernel(flags, here, diags, out, state, k_ref, yx_ref):
    width = k_ref.shape[1]
    lead = (flags[1] == 0) & (flags[2] == 0)

    @pl.when(lead)
    def _():
        prior = prior_of(diags[...])
        left = Part(None, prior[:width], None, prior[width:])
        var = diags[1:2]
        left = left._replace(diag=(columns(var)[:, :1], var))
        join([(left, parts(here[...]))], [state], k_ref, yx_ref, full=False)
        out[:width] = -eye_of(width)
        out[width : 2 * width] = state[:width]
        out[2 * width : 3 * width] = jnp.zeros((width, width), F32)
        out[3 * width :] = state[width:]

    @pl.when(jnp.logical_not(lead))
    def _():
        out[...] = here[...]


def pack(state, out):
    width = state.shape[1]
    half = width // 2
    rows = lax.broadcasted_iota(jnp.int32, (half, half), 0)
    lanes = lax.broadcasted_iota(jnp.int32, (half, half), 1)
    second = state[half:width, half:]
    diagonal = jnp.sum(jnp.where(rows == lanes, second, 0.0), axis=0, keepdims=True)
    out[:half, :half] = jnp.where(rows <= lanes, state[:half, :half], second)
    out[:half, half:] = state[:half, half:]
    tail = state[width:]
    at = lax.broadcasted_iota(jnp.int32, tail.shape, 0)
    diagonal = jnp.concatenate([diagonal, jnp.zeros_like(diagonal)], axis=1)
    out[half:] = jnp.where(at == 2, diagonal, tail)


def unpack(packed):
    width = packed.shape[1]
    half = width // 2
    rows = lax.broadcasted_iota(jnp.int32, (half, half), 0)
    lanes = lax.broadcasted_iota(jnp.int32, (half, half), 1)
    mixed, corner = packed[:half, :half], packed[:half, half:]
    turned = mixed.T
    first = jnp.where(rows <= lanes, mixed, turned)
    diagonal = packed[half + 2 : half + 3, :half]
    second = jnp.where(rows > lanes, mixed, jnp.where(rows < lanes, turned, diagonal))
    top = jnp.concatenate([first, corner], axis=1)
    bottom = jnp.concatenate([corner.T, second], axis=1)
    return jnp.concatenate([top, bottom]), packed[half:]


def total_kernel(full, flags, recv, own, out, *rest):
    k_ref, yx_ref = rest[-2:]

    @pl.when(flags[1] == 0)
    def _():
        later = flags[3] == 1
        there, here = recv[...], own[...]
        left = parts(jnp.where(later, there, here))
        right = parts(jnp.where(later, here, there))
        if full:
            join([(left, right)], [out], k_ref, yx_ref)
        else:
            (state,) = rest[:-2]
            join([(left, right)], [state], k_ref, yx_ref, full=False)
            pack(state, out)

    @pl.when(flags[1] != 0)
    def _():
        out[...] = jnp.zeros_like(out)


def block_target_kernel(flags, keep, recv, here, there, a, b, out_a, out_b, ahead, k_ref, yx_ref):
    half, core = flags[0] >> 1, flags[1]
    before = jnp.where(half == 1, jnp.where(core == 0, here[...], there[...]), 0.0)
    near = jnp.where(core == half, keep[...], recv[...])
    join([(parts(before), parts(near))], [ahead], k_ref, yx_ref)
    left = parts(ahead[...])
    first = parts(a[...])._replace(a=None, c=None)
    join([(left, first), (left, parts(b[...]))], [out_a, out_b], k_ref, yx_ref)


def target_kernel(flags, mine, other, a, b, out_a, out_b, k_ref, yx_ref):
    @pl.when(flags[3] == 1)
    def _():
        left = parts(jnp.where(flags[1] == 0, mine[...], other[...]))
        join([(left, parts(a[...])), (left, parts(b[...]))], [out_a, out_b], k_ref, yx_ref)

    @pl.when(flags[3] == 0)
    def _():
        out_a[...] = a[...]
        out_b[...] = b[...]


def final_kernel(flags, mine, other, diags, a, b, mean, cov, out_a, out_b, k_ref, yx_ref):
    width = k_ref.shape[1]
    cov_in, tail = unpack(jnp.where(flags[1] == 0, mine[...], other[...]))
    prior = prior_of(diags[...])
    early = flags[3] == 0
    left = Part(
        None, jnp.where(early, prior[:width], cov_in), None, jnp.where(early, prior[width:], tail)
    )
    join(
        [(left, parts(a[...])), (left, parts(b[...]))],
        [out_a, out_b],
        k_ref,
        yx_ref,
        full=False,
    )
    for i, out in enumerate((out_a, out_b)):
        cov[i] = out[:width]
        mean[i : i + 1] = out[width : width + 1]


def shards(
    observations,
    obs_precision,
    obs_values,
    obs_pattern,
    mix_values,
    trans_pattern,
    decay_rate,
    process_var,
    prior_mean,
    prior_var,
):
    units, width = obs_values.shape
    element = (3 * width + TAIL, width)
    state = (width + TAIL, width)
    count = lax.axis_size("outer") * lax.axis_size("inner")
    levels = int(math.log2(count))
    place = lax.axis_index("outer") * lax.axis_size("inner") + lax.axis_index("inner")
    cube = 2 * width**3
    evens = range(0, count, 2)
    across = [(i, i + 1) for i in evens]

    def flags_of(first):
        return jnp.stack([(place >> 1) & 3, place & 1, place >> 3, first])

    rows = jnp.concatenate([observations, obs_precision])
    received = []
    for turn in range(4):
        moves = []
        for i in range(count):
            at = i % 8
            moves.append((i, i - at + 2 * ((at & 3) ^ turn) + (at >> 2)))
        received.append(lax.ppermute(rows, AXES, moves))

    diags = jnp.stack([process_var, prior_var, prior_mean, decay_rate])
    high, low, turned, trans = call(
        prep_kernel,
        "prep",
        [((units, width), BF16), ((units, width), BF16), (width, units), (width, width)],
        [obs_pattern, trans_pattern, obs_values, mix_values, diags],
        0,
        width,
        4 * cube,
        scalars=2,
        extra=[
            pltpu.VMEM((units, width), F32),
            pltpu.VMEM((width, width), F32),
            pltpu.SemaphoreType.DMA((5,)),
        ],
        placed=(2, 3),
    )
    model = [high, low, turned, trans, diags]
    received, model = lax.optimization_barrier((received, model))
    flags = flags_of(place & 1)
    here, keep, send = call(
        half_kernel,
        "half",
        [element] * 3,
        [flags, *received, *model],
        4,
        width,
        150 * cube,
        scalars=1,
        extra=[
            pltpu.VMEM((4, 4, units), F32),
            pltpu.VMEM((4,) + element, F32),
            pltpu.VMEM((2,) + element, F32),
            pltpu.VMEM((2,) + element, F32),
            pltpu.VMEM((8, width, width), F32),
            pltpu.VMEM((32, width), F32),
        ],
    )
    cores = [(i, i ^ 1) for i in range(count)]
    there = lax.ppermute(here, AXES, cores)
    (total,) = call(
        start_kernel,
        "start",
        [element],
        [flags, here, diags],
        0,
        width,
        10 * cube,
        scalars=1,
        extra=[pltpu.VMEM(state, F32)] + scratch(1, width),
    )
    there, total = lax.optimization_barrier((there, total))
    send, there = lax.optimization_barrier((send, there))
    recv = lax.ppermute(send, AXES, cores)
    packed = (width // 2 + TAIL, width)
    for level in range(2, levels - 1):
        full = level < levels - 2
        if level == 2:
            incoming = there
        else:
            incoming = mine
            flags = flags_of((place >> level) & 1)
        (total,) = call(
            functools.partial(total_kernel, full),
            "total",
            [element if full else packed],
            [flags, incoming, total],
            0,
            width,
            15 * cube,
            scalars=1,
            extra=([] if full else [pltpu.VMEM(state, F32)]) + scratch(1, width),
        )
        step = 2 << level
        if full:
            mine = lax.ppermute(total, AXES, [(i, i ^ step) for i in evens])
        else:
            early = [i for i in evens if i < step]
            mine = lax.ppermute(total, AXES, [(i, i ^ step) for i in early])
            other = lax.ppermute(total, AXES, [(i, (i ^ step) + 1) for i in early])
        if level == 2:
            targets = call(
                own_kernel, "own", [element] * 2, [rows, *model], 1, width, 30 * cube
            )
            targets = call(
                block_target_kernel,
                "block_targets",
                [element] * 2,
                [flags, keep, recv, here, there, *targets],
                0,
                width,
                45 * cube,
                scalars=1,
                extra=[pltpu.VMEM(element, F32)] + scratch(2, width),
            )
        else:
            targets = call(
                target_kernel,
                "targets",
                [element] * 2,
                [flags, *held, *targets],
                2,
                width,
                30 * cube,
                scalars=1,
            )
        mine, targets = lax.optimization_barrier((mine, targets))
        if full:
            held = (mine, lax.ppermute(mine, AXES, across))
    return call(
        final_kernel,
        "final",
        [(2, width), (2, width, width)],
        [flags_of(place >> (levels - 1)), mine, other, diags, *targets],
        0,
        width,
        30 * cube,
        scalars=1,
        extra=[pltpu.VMEM(state, F32)] * 2 + scratch(2, width),
    )


def solution(mesh):
    split = P(AXES, None)
    in_specs = (split, split) + (P(),) * 8
    out_specs = (split, P(AXES, None, None))
    return jax.shard_map(shards, mesh=mesh, in_specs=in_specs, out_specs=out_specs, check_vma=False)
```

```python
import collections
import functools
import math

import jax
import jax.numpy as jnp
from jax import lax
from jax.experimental import pallas as pl
from jax.experimental.pallas import tpu as pltpu
from jax.sharding import PartitionSpec as P

BLOCK = 64
TAIL = 16
AXES = ("outer", "inner")
F32 = jnp.float32
BF16 = jnp.bfloat16


Part = collections.namedtuple("Part", "a c j v diag", defaults=(None,))


def dot(left, right, contract=((1,), (0,))):
    return lax.dot_general(
        left,
        right,
        (contract, ((), ())),
        precision=lax.Precision.HIGH,
        preferred_element_type=F32,
    )


def dot_rt(left, right):
    return dot(left, right, ((1,), (1,)))


def eye_of(width):
    rows = lax.broadcasted_iota(jnp.int32, (width, width), 0)
    cols = lax.broadcasted_iota(jnp.int32, (width, width), 1)
    return jnp.where(rows == cols, 1.0, 0.0).astype(F32)


def tail_row(tail, source, target):
    rows = lax.broadcasted_iota(jnp.int32, tail.shape, 0)
    return jnp.where(rows == target, jnp.broadcast_to(tail[source : source + 1], tail.shape), 0.0)


def parts(value):
    width = value.shape[1]
    return Part(
        value[:width], value[width : 2 * width], value[2 * width : 3 * width], value[3 * width :]
    )


def invert(size, k_ref, yx_ref, norm):
    width = k_ref.shape[1]
    batch = range(size)
    tiny = norm <= 1e-2
    small = jnp.logical_and(norm <= 5e-2, jnp.logical_not(tiny))

    @pl.when(tiny)
    def _():
        for b in batch:
            yx_ref[b, :width] = k_ref[b] - yx_ref[b, :width]

    @pl.when(small)
    def _():
        for b in batch:
            squared = yx_ref[b, :width]
            begun = k_ref[b] - squared
            yx_ref[b, :width] = begun + dot(begun, squared)

    @pl.when(norm > 5e-2)
    def _():
        iterate(size, k_ref, yx_ref, norm)


def iterate(size, k_ref, yx_ref, norm):
    width = k_ref.shape[1]
    batch = range(size)
    rho = norm / (2.0 + norm)
    alpha = 2.0 / (2.0 + norm)
    scale = 2.0 / (2.0 - rho * rho)
    ident = eye_of(width)
    for b in batch:
        k = k_ref[b]
        squared = yx_ref[b, :width]
        first = alpha * (ident + k)
        second = (alpha * alpha) * (ident + 2.0 * k + squared)
        yx_ref[b, :width] = scale * (2.0 * first - second)
        yx_ref[b, width:] = (scale * alpha) * (2.0 * ident - first)

    def step(rho):
        scale = 2.0 / (2.0 - rho * rho)
        for b in batch:
            both = yx_ref[b]
            yx_ref[b] = scale * (2.0 * both - dot(both, both[:width]))
        return rho * rho / (2.0 - rho * rho)

    lax.while_loop(lambda r: r > 3e-3, step, rho * rho / (2.0 - rho * rho))
    rests = []
    for b in batch:
        x = yx_ref[b, width:]
        rests.append(ident - x - dot(k_ref[b], x))
    for b in batch:
        x = yx_ref[b, width:]
        yx_ref[b, :width] = ident - x - dot(x, rests[b])


def join(pairs, outs, k_ref, yx_ref, full=True):
    width = k_ref.shape[1]
    batch = range(len(pairs))
    for b in batch:
        left, right = pairs[b]
        k_ref[b] = left.diag[0] * right.j if left.diag else dot(left.c, right.j)
    sums = []
    for b in batch:
        squared = dot(k_ref[b], k_ref[b])
        yx_ref[b, :width] = squared
        sums.append(jnp.sum(squared * squared))
    norm = jnp.sqrt(jnp.sqrt(functools.reduce(jnp.maximum, sums)))
    hus, ngs = [], []
    for b in batch:
        left, right = pairs[b]
        stack = right.v if right.a is None else jnp.concatenate([right.a, right.v])
        h = stack * left.diag[1] if left.diag else dot(stack, left.c)
        u = tail_row(left.v, 0, 0) + tail_row(h[-TAIL:], 1, 0)
        h = left.c if right.a is None else h[:width] + left.c
        hus.append(jnp.concatenate([h, u]))
        if full:
            n = dot(jnp.concatenate([left.a.T, left.v]), right.j)
            g = tail_row(right.v, 1, 1) - tail_row(n[width:], 0, 1)
            ngs.append(jnp.concatenate([n[:width] + right.j, g]))
    invert(len(pairs), k_ref, yx_ref, norm)
    ws, vs = [], []
    for b in batch:
        right = pairs[b][1]
        z = yx_ref[b, :width]
        ws.append(-z if right.a is None else right.a - z - dot(right.a, z))
    if full:
        for b in batch:
            left = pairs[b][0]
            z = yx_ref[b, :width]
            vs.append(left.a - z - dot(z, left.a))
    for b in batch:
        left, right = pairs[b]
        cb = hus[b] + dot_rt(hus[b], ws[b])
        c = cb[:width] if right.c is None else cb[:width] + right.c
        tail = cb[width:] + tail_row(right.v, 0, 0)
        if full:
            je = ngs[b] + dot(ngs[b], vs[b])
            tail = tail + je[width:] + tail_row(left.v, 1, 1)
            if right.a is None:
                outs[b][:width] = vs[b]
            else:
                outs[b][:width] = dot(ws[b], left.a) + ws[b] + left.a
            outs[b][2 * width : 3 * width] = je[:width] + left.j
            outs[b][width : 2 * width] = c
            outs[b][3 * width :] = tail
        else:
            outs[b][0][...] = c
            outs[b][1][...] = tail


def state_of(ref):
    width = ref.shape[1]
    return ref.at[:width], ref.at[width:]


def scratch(size, width):
    return [pltpu.VMEM((size, width, width), F32), pltpu.VMEM((size, 2 * width, width), F32)]


def call(kernel, name, outs, ins, size, width, flops, scalars=0, extra=(), limit=12, apart=False):
    smem = pl.BlockSpec(memory_space=pltpu.SMEM)
    vmem = pl.BlockSpec(memory_space=pltpu.VMEM)
    away = pl.BlockSpec(memory_space=pltpu.HBM)
    shapes = [o if isinstance(o[0], tuple) else (o, F32) for o in outs]
    return pl.pallas_call(
        kernel,
        name=name,
        out_shape=[jax.ShapeDtypeStruct(*o) for o in shapes],
        in_specs=[smem] * scalars + [away if apart else vmem] * (len(ins) - scalars),
        out_specs=[vmem] * len(outs),
        scratch_shapes=list(extra) + (scratch(size, width) if size else []),
        compiler_params=pltpu.CompilerParams(vmem_limit_bytes=limit << 20),
        cost_estimate=pl.CostEstimate(flops=flops, bytes_accessed=4 << 20, transcendentals=0),
    )(*ins)


def block_rows(pattern, width):
    lanes = lax.broadcasted_iota(jnp.int32, (pattern.shape[0], width), 1) // BLOCK
    out = jnp.zeros((pattern.shape[0], width), F32)
    for col in range(width // BLOCK):
        out = jnp.where(lanes == col, pattern[:, col : col + 1].astype(F32), out)
    return out


def columns(rows):
    width = rows.shape[1]
    return jnp.concatenate([rows, jnp.zeros((8 - rows.shape[0], width), F32)]).T


def gram_of(weight, high, low, turned):
    scaled = turned[...] * weight
    top = scaled.astype(BF16)
    rest = (scaled - top.astype(F32)).astype(BF16)
    part = functools.partial(jnp.dot, preferred_element_type=F32)
    return part(top, high[...]) + (part(top, low[...]) + part(rest, high[...]))


def update_of(gram, score):
    rows = lax.broadcasted_iota(jnp.int32, (TAIL, gram.shape[0]), 0)
    return Part(None, None, gram, jnp.where(rows == 1, score, 0.0))


def step_of(gram, score, trans, var):
    width = gram.shape[0]
    return update_of(gram, score)._replace(
        a=trans, c=eye_of(width) * var[0], diag=(var[1], var[0])
    )


def scores_of(rows, turned):
    product = rows[:2] * rows[2:4]
    return dot_rt(jnp.concatenate([product, jnp.zeros((6, rows.shape[1]), F32)]), turned[...])


def prior_of(diags):
    width = diags.shape[1]
    rows = lax.broadcasted_iota(jnp.int32, (TAIL, width), 0)
    return jnp.concatenate(
        [eye_of(width) * diags[1:2], jnp.where(rows == 0, diags[2:3], 0.0)]
    )


def prep_kernel(*refs):
    ins, (high, low, turned, trans, diags) = refs[:8], refs[8:13]
    values, mix, obs_pattern, trans_pattern, vectors, sems = refs[13:]
    count, width = values.shape
    pieces = 4
    piece = count // pieces
    pairs = [(ins[0], obs_pattern), (ins[1], trans_pattern), (ins[3], mix)]
    pairs += [(ins[4 + i], vectors.at[i]) for i in range(4)]
    for i in range(pieces):
        rows = pl.ds(i * piece, piece)
        pairs.append((ins[2].at[rows], values.at[rows]))
    copies = [pltpu.make_async_copy(*pairs[i], sems.at[i]) for i in range(len(pairs))]
    for copy in copies:
        copy.start()
    for copy in copies[: len(pairs) - pieces]:
        copy.wait()
    for i in range(4):
        diags[i : i + 1] = vectors[i]
    obs_rows = block_rows(obs_pattern[...].T, width)
    trans_rows = block_rows(trans_pattern[...], width)
    for i in range(count // BLOCK):
        if i * BLOCK % piece == 0:
            copies[len(pairs) - pieces + i * BLOCK // piece].wait()
        rows = pl.ds(i * BLOCK, BLOCK)
        block = values[rows] * obs_rows[i : i + 1]
        high[rows] = block.astype(BF16)
        low[rows] = (block - high[rows].astype(F32)).astype(BF16)
        turned[:, rows] = block.T
    decay = columns(diags[3:4])[:, :1]
    for i in range(width // BLOCK):
        rows = pl.ds(i * BLOCK, BLOCK)
        row_at = lax.broadcasted_iota(jnp.int32, (BLOCK, width), 0) + i * BLOCK
        lanes = lax.broadcasted_iota(jnp.int32, (BLOCK, width), 1)
        mask = jnp.where(lanes // BLOCK == i, 1.0, trans_rows[i : i + 1])
        coupling = jnp.where(row_at == lanes, 0.0, mix[rows] * mask)
        row_abs = jnp.sum(jnp.abs(coupling), axis=1, keepdims=True) + 1e-06
        retain = jnp.exp(-decay[i * BLOCK : (i + 1) * BLOCK])
        trans[rows] = jnp.where(
            row_at == lanes, retain - 1.0, (0.95 * (1.0 - retain) / row_abs) * coupling
        )


def half_kernel(flags, *refs):
    ins, (high, low, turned, trans, diags, total, keep, send, start) = refs[:2], refs[2:11]
    rows_ref, elements, quads, ahead, grams, scores, k_ref, yx_ref = refs[11:]
    width = trans.shape[0]
    chip, core = flags[0], flags[1]
    for slot in range(2):
        rows_ref[slot] = ins[slot][...]
    for j in range(4):
        rows_v = rows_ref[(chip & 1) ^ (j >> 1), (chip >> 1) ^ (j & 1)]
        scores[8 * j : 8 * j + 8] = scores_of(rows_v, turned)
        for i in range(2):
            grams[2 * j + i] = gram_of(rows_v[2 + i : 3 + i], high, low, turned)
    var = diags[0:1]
    var = (var, columns(var)[:, :1])
    t = trans[...]
    pairs = []
    for j in range(4):
        pairs.append(
            tuple(
                step_of(grams[2 * j + i], scores[8 * j + i : 8 * j + i + 1], t, var)
                for i in range(2)
            )
        )
    join(pairs, [elements.at[j] for j in range(4)], k_ref, yx_ref)
    join(
        [(parts(elements[2 * i]), parts(elements[2 * i + 1])) for i in range(2)],
        [quads.at[i] for i in range(2)],
        k_ref,
        yx_ref,
    )
    odd = chip & 1
    both = (parts(quads[0]), parts(quads[1]))
    near = core == chip >> 1
    ahead[0] = jnp.where(odd == 1, quads[0], 0.0)
    first = (parts(ahead[0]), parts(elements[2 * odd]))
    join([both, first], [total, ahead.at[1]], k_ref, yx_ref)

    @pl.when(near)
    def _():
        own = []
        for i in range(2):
            j = 2 * odd + i
            rows_v = scores[pl.ds(pl.multiple_of(8 * j, 8), 8)]
            updates = [update_of(grams[2 * j + n], rows_v[n : n + 1]) for n in range(2)]
            left = step_of(updates[0].j, rows_v[:1], trans[...], var)
            own.append((left, updates[1]))
        size = total.shape[0]
        join(own, [elements.at[i] for i in range(2)], k_ref, yx_ref)
        for i, out in ((core, keep), (1 - core, send)):
            j = 2 * odd + i
            rows_v = scores[pl.ds(pl.multiple_of(8 * j, 8), 8)]
            update = update_of(grams[2 * j], rows_v[:1])
            out[:size] = ahead[i]
            out[size : 2 * size] = elements[i]
            out[2 * size : 2 * size + width] = update.j
            out[2 * size + width :] = update.v

    lead = (core == 0) & (flags[2] == 0)

    @pl.when(lead)
    def _():
        prior = prior_of(diags[...])
        var = diags[1:2]
        left = Part(None, prior[:width], None, prior[width:], (columns(var)[:, :1], var))
        join([(left, parts(total[...]))], [state_of(start)], k_ref, yx_ref, full=False)

    @pl.when(jnp.logical_not(lead))
    def _():
        start[...] = jnp.zeros_like(start)


def pack(state, out):
    width = state.shape[1]
    half = width // 2
    rows = lax.broadcasted_iota(jnp.int32, (half, half), 0)
    lanes = lax.broadcasted_iota(jnp.int32, (half, half), 1)
    second = state[half:width, half:]
    diagonal = jnp.sum(jnp.where(rows == lanes, second, 0.0), axis=0, keepdims=True)
    out[:half, :half] = jnp.where(rows <= lanes, state[:half, :half], second)
    out[:half, half:] = state[:half, half:]
    tail = state[width:]
    at = lax.broadcasted_iota(jnp.int32, tail.shape, 0)
    diagonal = jnp.concatenate([diagonal, jnp.zeros_like(diagonal)], axis=1)
    out[half:] = jnp.where(at == 2, diagonal, tail)


def unpack(packed):
    width = packed.shape[1]
    half = width // 2
    rows = lax.broadcasted_iota(jnp.int32, (half, half), 0)
    lanes = lax.broadcasted_iota(jnp.int32, (half, half), 1)
    mixed, corner = packed[:half, :half], packed[:half, half:]
    turned = mixed.T
    first = jnp.where(rows <= lanes, mixed, turned)
    diagonal = packed[half + 2 : half + 3, :half]
    second = jnp.where(rows > lanes, mixed, jnp.where(rows < lanes, turned, diagonal))
    top = jnp.concatenate([first, corner], axis=1)
    bottom = jnp.concatenate([corner.T, second], axis=1)
    return jnp.concatenate([top, bottom]), packed[half:]


def pack_element(element, out):
    width = element.shape[1]
    rows = lax.broadcasted_iota(jnp.int32, (width, width), 0)
    lanes = lax.broadcasted_iota(jnp.int32, (width, width), 1)
    c, j = element[width : 2 * width], element[2 * width : 3 * width]
    out[:width] = element[:width]
    out[width : 2 * width] = jnp.where(rows <= lanes, c, j)
    tail = element[3 * width :]
    diagonal = jnp.sum(jnp.where(rows == lanes, j, 0.0), axis=0, keepdims=True)
    at = lax.broadcasted_iota(jnp.int32, tail.shape, 0)
    out[2 * width :] = jnp.where(at == 2, diagonal, tail)


def unpack_element(packed):
    width = packed.shape[1]
    rows = lax.broadcasted_iota(jnp.int32, (width, width), 0)
    lanes = lax.broadcasted_iota(jnp.int32, (width, width), 1)
    mixed, tail = packed[width : 2 * width], packed[2 * width :]
    turned = mixed.T
    c = jnp.where(rows <= lanes, mixed, turned)
    j = jnp.where(rows > lanes, mixed, jnp.where(rows < lanes, turned, tail[2:3]))
    return Part(packed[:width], c, j, tail)


def total_kernel(full, begins, flags, recv, own, *rest):
    *rest, k_ref, yx_ref = rest
    begin, (out, *state) = rest[:begins], rest[begins:]
    sent = (flags[1] == 0) & (full | (flags[4] == 0))

    @pl.when(sent)
    def _():
        later = flags[3] == 1
        there, here = recv[...], own[...]
        if begin:
            (start,) = begin
            width = start.shape[1]
            zero = jnp.zeros((width, width), F32)
            begun = jnp.concatenate([-eye_of(width), start[:width], zero, start[width:]])
            here = jnp.where(flags[2] == 0, begun, here)
        split = parts if begins else unpack_element
        left = split(jnp.where(later, there, here))
        right = split(jnp.where(later, here, there))
        outs = [state[0]] if full else [state_of(state[0])]
        join([(left, right)], outs, k_ref, yx_ref, full)
        (pack_element if full else pack)(state[0], out)

    @pl.when(jnp.logical_not(sent))
    def _():
        out[...] = jnp.zeros_like(out)


def block_target_kernel(flags, keep, recv, here, there, out_a, out_b, ahead, k_ref, yx_ref):
    half, core = flags[0] >> 1, flags[1]
    size, width = here.shape
    own = core == half
    pick = lambda start, end: jnp.where(own, keep[start:end], recv[start:end])
    before = jnp.where(half == 1, jnp.where(core == 0, here[...], there[...]), 0.0)
    join([(parts(before), parts(pick(0, size)))], [ahead], k_ref, yx_ref)
    left = parts(ahead[...])
    end = 2 * size + width
    first = Part(None, None, pick(2 * size, end), pick(end, keep.shape[0]))
    join(
        [(left, first), (left, parts(pick(size, 2 * size)))], [out_a, out_b], k_ref, yx_ref
    )


def target_kernel(flags, mine, other, a, b, out_a, out_b, k_ref, yx_ref):
    def after(outs, full):
        left = unpack_element(jnp.where(flags[1] == 0, mine[...], other[...]))
        join([(left, parts(a[...])), (left, parts(b[...]))], outs, k_ref, yx_ref, full)

    first = flags[5] == 1

    @pl.when((flags[3] == 1) & jnp.logical_not(first))
    def _():
        after([out_a, out_b], True)

    @pl.when((flags[3] == 1) & first)
    def _():
        width = k_ref.shape[1]
        for out in (out_a, out_b):
            out[:width] = -eye_of(width)
            out[2 * width : 3 * width] = jnp.zeros((width, width), F32)
        after([(o.at[width : 2 * width], o.at[3 * width :]) for o in (out_a, out_b)], False)

    @pl.when(flags[3] == 0)
    def _():
        out_a[...] = a[...]
        out_b[...] = b[...]


def final_kernel(flags, mine, other, diags, a, b, mean, cov, out_a, out_b, k_ref, yx_ref):
    width = k_ref.shape[1]
    early = flags[4] == 0
    done = early & (flags[2] > 0)
    outs = (out_a, out_b)

    @pl.when(jnp.logical_not(done))
    def _():
        cov_in, tail = unpack(jnp.where(flags[1] == 0, mine[...], other[...]))
        prior = prior_of(diags[...])
        cov_in = jnp.where(early, prior[:width], cov_in)
        left = Part(None, cov_in, None, jnp.where(early, prior[width:], tail))
        states = [state_of(out) for out in outs]
        join([(left, parts(a[...])), (left, parts(b[...]))], states, k_ref, yx_ref, full=False)

    @pl.when(done)
    def _():
        for target, out in zip((a, b), outs):
            out[:width] = target[width : 2 * width]
            out[width:] = target[3 * width :]

    for i, out in enumerate(outs):
        cov[i] = out[:width]
        mean[i : i + 1] = out[width : width + 1]


def shards(
    observations,
    obs_precision,
    obs_values,
    obs_pattern,
    mix_values,
    trans_pattern,
    decay_rate,
    process_var,
    prior_mean,
    prior_var,
):
    units, width = obs_values.shape
    element = (3 * width + TAIL, width)
    state = (width + TAIL, width)
    ahead = (2 * element[0] + width + TAIL, width)
    link = (2 * width + TAIL, width)
    count = lax.axis_size("outer") * lax.axis_size("inner")
    levels = int(math.log2(count))
    place = lax.axis_index("outer") * lax.axis_size("inner") + lax.axis_index("inner")
    cube = 2 * width**3
    evens = range(0, count, 2)
    across = [(i, i + 1) for i in evens]

    def flags_of(first, level=2):
        begun = ((place >> (level + 1)) == 0).astype(place.dtype)
        return jnp.stack([(place >> 1) & 3, place & 1, place >> 3, first, place >> (levels - 1), begun])

    cores = [(i, i ^ 1) for i in range(count)]
    rows = jnp.concatenate([observations, obs_precision])
    beside = lax.ppermute(rows, AXES, cores)
    pair = jnp.stack([rows, beside])
    received = []
    for turn in range(2):
        moves = []
        for i in range(count):
            chip = i % 8 // 2
            goal = 2 * (i & 1) + (turn ^ (chip & 1))
            moves.append((i, i - i % 8 + 2 * goal + (chip >> 1)))
        received.append(lax.ppermute(pair, AXES, moves))
    vectors = [v[None] for v in (process_var, prior_var, prior_mean, decay_rate)]
    shape = obs_pattern.shape
    model = call(
        prep_kernel,
        "prep",
        [((units, width), BF16), ((units, width), BF16), (width, units), (width, width), (4, width)],
        [obs_pattern.T, trans_pattern, obs_values, mix_values, *vectors],
        0,
        width,
        4 * cube,
        extra=[
            pltpu.VMEM((units, width), F32),
            pltpu.VMEM((width, width), F32),
            pltpu.VMEM(shape[::-1], jnp.int32),
            pltpu.VMEM(trans_pattern.shape, jnp.int32),
            pltpu.VMEM((4, 1, width), F32),
            pltpu.SemaphoreType.DMA((11,)),
        ],
        apart=True,
    )
    diags = model[-1]
    received, model = lax.optimization_barrier((received, model))
    flags = flags_of(place & 1)
    here, keep, send, start = call(
        half_kernel,
        "half",
        [element, ahead, ahead, state],
        [flags, *received, *model],
        4,
        width,
        150 * cube,
        scalars=1,
        extra=[
            pltpu.VMEM((2, 2, 4, units), F32),
            pltpu.VMEM((4,) + element, F32),
            pltpu.VMEM((2,) + element, F32),
            pltpu.VMEM((2,) + element, F32),
            pltpu.VMEM((8, width, width), F32),
            pltpu.VMEM((32, width), F32),
        ],
        limit=32,
    )
    there = lax.ppermute(here, AXES, cores)
    send, there = lax.optimization_barrier((send, there))
    recv = lax.ppermute(send, AXES, cores)
    packed = (width // 2 + TAIL, width)
    total = here
    for level in range(2, levels - 1):
        full = level < levels - 2
        if level == 2:
            incoming = there
        else:
            incoming = mine
            flags = flags_of((place >> level) & 1, level)
        (total,) = call(
            functools.partial(total_kernel, full, int(level == 2)),
            "total",
            [link if full else packed],
            [flags, incoming, total] + ([start] if level == 2 else []),
            0,
            width,
            15 * cube,
            scalars=1,
            extra=[pltpu.VMEM(element if full else state, F32)] + scratch(1, width),
        )
        step = 2 << level
        if full:
            mine = lax.ppermute(total, AXES, [(i, i ^ step) for i in evens])
        else:
            early = [i for i in evens if i < step]
            mine = lax.ppermute(total, AXES, [(i, i ^ step) for i in early])
            other = lax.ppermute(total, AXES, [(i, (i ^ step) + 1) for i in early])
        if level > 2:
            incoming, total = lax.optimization_barrier((incoming, total))
            held = (incoming, lax.ppermute(incoming, AXES, across))
        if level == 2:
            targets = call(
                block_target_kernel,
                "block_targets",
                [element] * 2,
                [flags, keep, recv, here, there],
                0,
                width,
                45 * cube,
                scalars=1,
                extra=[pltpu.VMEM(element, F32)] + scratch(2, width),
            )
        else:
            targets = call(
                target_kernel,
                "targets",
                [element] * 2,
                [flags, *held, *targets],
                2,
                width,
                30 * cube,
                scalars=1,
            )
        mine, targets = lax.optimization_barrier((mine, targets))
    return call(
        final_kernel,
        "final",
        [(2, width), (2, width, width)],
        [flags, mine, other, diags, *targets],
        0,
        width,
        30 * cube,
        scalars=1,
        extra=[pltpu.VMEM(state, F32)] * 2 + scratch(2, width),
    )


def solution(mesh):
    split = P(AXES, None)
    in_specs = (split, split) + (P(),) * 8
    out_specs = (split, P(AXES, None, None))
    return jax.shard_map(shards, mesh=mesh, in_specs=in_specs, out_specs=out_specs, check_vma=False)
```

```python
import collections
import functools
import math

import jax
import jax.numpy as jnp
from jax import lax
from jax.experimental import pallas as pl
from jax.experimental.pallas import tpu as pltpu
from jax.sharding import PartitionSpec as P

BLOCK = 64
TAIL = 16
AXES = ("outer", "inner")
F32 = jnp.float32
BF16 = jnp.bfloat16


Part = collections.namedtuple("Part", "a c j v diag", defaults=(None,))


def dot(left, right, contract=((1,), (0,))):
    return lax.dot_general(
        left,
        right,
        (contract, ((), ())),
        precision=lax.Precision.HIGH,
        preferred_element_type=F32,
    )


def dot_rt(left, right):
    return dot(left, right, ((1,), (1,)))


def eye_of(width):
    rows = lax.broadcasted_iota(jnp.int32, (width, width), 0)
    cols = lax.broadcasted_iota(jnp.int32, (width, width), 1)
    return jnp.where(rows == cols, 1.0, 0.0).astype(F32)


def tail_row(tail, source, target):
    rows = lax.broadcasted_iota(jnp.int32, tail.shape, 0)
    return jnp.where(rows == target, jnp.broadcast_to(tail[source : source + 1], tail.shape), 0.0)


def parts(value):
    width = value.shape[1]
    return Part(
        value[:width], value[width : 2 * width], value[2 * width : 3 * width], value[3 * width :]
    )


def invert(size, k_ref, yx_ref, norm):
    width = k_ref.shape[1]
    batch = range(size)
    tiny = norm <= 1e-2
    small = jnp.logical_and(norm <= 5e-2, jnp.logical_not(tiny))

    @pl.when(tiny)
    def _():
        for b in batch:
            yx_ref[b, :width] = k_ref[b] - yx_ref[b, :width]

    @pl.when(small)
    def _():
        for b in batch:
            squared = yx_ref[b, :width]
            begun = k_ref[b] - squared
            yx_ref[b, :width] = begun + dot(begun, squared)

    @pl.when(norm > 5e-2)
    def _():
        iterate(size, k_ref, yx_ref, norm)


def iterate(size, k_ref, yx_ref, norm):
    width = k_ref.shape[1]
    batch = range(size)
    rho = norm / (2.0 + norm)
    alpha = 2.0 / (2.0 + norm)
    scale = 2.0 / (2.0 - rho * rho)
    ident = eye_of(width)
    for b in batch:
        k = k_ref[b]
        squared = yx_ref[b, :width]
        first = alpha * (ident + k)
        second = (alpha * alpha) * (ident + 2.0 * k + squared)
        yx_ref[b, :width] = scale * (2.0 * first - second)
        yx_ref[b, width:] = (scale * alpha) * (2.0 * ident - first)

    def step(rho):
        scale = 2.0 / (2.0 - rho * rho)
        for b in batch:
            both = yx_ref[b]
            yx_ref[b] = scale * (2.0 * both - dot(both, both[:width]))
        return rho * rho / (2.0 - rho * rho)

    lax.while_loop(lambda r: r > 3e-3, step, rho * rho / (2.0 - rho * rho))
    rests = []
    for b in batch:
        x = yx_ref[b, width:]
        rests.append(ident - x - dot(k_ref[b], x))
    for b in batch:
        x = yx_ref[b, width:]
        yx_ref[b, :width] = ident - x - dot(x, rests[b])


def join(pairs, outs, k_ref, yx_ref, full=True):
    width = k_ref.shape[1]
    batch = range(len(pairs))
    for b in batch:
        left, right = pairs[b]
        k_ref[b] = left.diag[0] * right.j if left.diag else dot(left.c, right.j)
    sums = []
    for b in batch:
        squared = dot(k_ref[b], k_ref[b])
        yx_ref[b, :width] = squared
        sums.append(jnp.sum(squared * squared))
    norm = jnp.sqrt(jnp.sqrt(functools.reduce(jnp.maximum, sums)))
    hus, ngs = [], []
    for b in batch:
        left, right = pairs[b]
        stack = right.v if right.a is None else jnp.concatenate([right.a, right.v])
        h = stack * left.diag[1] if left.diag else dot(stack, left.c)
        u = tail_row(left.v, 0, 0) + tail_row(h[-TAIL:], 1, 0)
        h = left.c if right.a is None else h[:width] + left.c
        hus.append(jnp.concatenate([h, u]))
        if full:
            n = dot(jnp.concatenate([left.a.T, left.v]), right.j)
            g = tail_row(right.v, 1, 1) - tail_row(n[width:], 0, 1)
            ngs.append(jnp.concatenate([n[:width] + right.j, g]))
    invert(len(pairs), k_ref, yx_ref, norm)
    ws, vs = [], []
    for b in batch:
        right = pairs[b][1]
        z = yx_ref[b, :width]
        ws.append(-z if right.a is None else right.a - z - dot(right.a, z))
    if full:
        for b in batch:
            left = pairs[b][0]
            z = yx_ref[b, :width]
            vs.append(left.a - z - dot(z, left.a))
    for b in batch:
        left, right = pairs[b]
        cb = hus[b] + dot_rt(hus[b], ws[b])
        c = cb[:width] if right.c is None else cb[:width] + right.c
        tail = cb[width:] + tail_row(right.v, 0, 0)
        if full:
            je = ngs[b] + dot(ngs[b], vs[b])
            tail = tail + je[width:] + tail_row(left.v, 1, 1)
            if right.a is None:
                outs[b][:width] = vs[b]
            else:
                outs[b][:width] = dot(ws[b], left.a) + ws[b] + left.a
            outs[b][2 * width : 3 * width] = je[:width] + left.j
            outs[b][width : 2 * width] = c
            outs[b][3 * width :] = tail
        else:
            outs[b][0][...] = c
            outs[b][1][...] = tail


def state_of(ref):
    width = ref.shape[1]
    return ref.at[:width], ref.at[width:]


def scratch(size, width):
    return [pltpu.VMEM((size, width, width), F32), pltpu.VMEM((size, 2 * width, width), F32)]


def call(kernel, name, outs, ins, size, width, flops, scalars=0, extra=(), limit=12):
    smem = pl.BlockSpec(memory_space=pltpu.SMEM)
    vmem = pl.BlockSpec(memory_space=pltpu.VMEM)
    shapes = [o if isinstance(o[0], tuple) else (o, F32) for o in outs]
    return pl.pallas_call(
        kernel,
        name=name,
        out_shape=[jax.ShapeDtypeStruct(*o) for o in shapes],
        in_specs=[smem] * scalars + [vmem] * (len(ins) - scalars),
        out_specs=[vmem] * len(outs),
        scratch_shapes=list(extra) + (scratch(size, width) if size else []),
        compiler_params=pltpu.CompilerParams(vmem_limit_bytes=limit << 20),
        cost_estimate=pl.CostEstimate(flops=flops, bytes_accessed=4 << 20, transcendentals=0),
    )(*ins)


def columns(rows):
    width = rows.shape[1]
    return jnp.concatenate([rows, jnp.zeros((8 - rows.shape[0], width), F32)]).T


def gram_of(weight, high, low, turned):
    scaled = turned[...] * weight
    top = scaled.astype(BF16)
    rest = (scaled - top.astype(F32)).astype(BF16)
    part = functools.partial(jnp.dot, preferred_element_type=F32)
    return part(top, high[...]) + (part(top, low[...]) + part(rest, high[...]))


def update_of(gram, score):
    rows = lax.broadcasted_iota(jnp.int32, (TAIL, gram.shape[0]), 0)
    return Part(None, None, gram, jnp.where(rows == 1, score, 0.0))


def step_of(gram, score, trans, var):
    width = gram.shape[0]
    return update_of(gram, score)._replace(
        a=trans, c=eye_of(width) * var[0], diag=(var[1], var[0])
    )


def scores_of(rows, turned):
    product = rows[:2] * rows[2:4]
    return dot_rt(jnp.concatenate([product, jnp.zeros((6, rows.shape[1]), F32)]), turned[...])


def prior_of(diags):
    width = diags.shape[1]
    rows = lax.broadcasted_iota(jnp.int32, (TAIL, width), 0)
    return jnp.concatenate(
        [eye_of(width) * diags[1:2], jnp.where(rows == 0, diags[2:3], 0.0)]
    )


def block_rows(pattern, width):
    lanes = lax.broadcasted_iota(jnp.int32, (pattern.shape[0], width), 1) // BLOCK
    out = jnp.zeros((pattern.shape[0], width), F32)
    for col in range(width // BLOCK):
        out = jnp.where(lanes == col, pattern[:, col : col + 1], out)
    return out


def prep_kernel(small, values, mix, high, low, turned, trans):
    count, width = values.shape
    blocks = width // BLOCK
    patterns = small[:8, :128].T
    obs_rows = block_rows(patterns[: count // BLOCK, 4:8], width)
    trans_rows = block_rows(patterns[count // BLOCK : count // BLOCK + blocks, 4:8], width)
    for i in range(count // BLOCK):
        rows = pl.ds(i * BLOCK, BLOCK)
        block = values[rows] * obs_rows[i : i + 1]
        high[rows] = block.astype(BF16)
        low[rows] = (block - high[rows].astype(F32)).astype(BF16)
        turned[:, rows] = block.T
    decay = columns(small[3:4])[:, :1]
    for i in range(blocks):
        rows = pl.ds(i * BLOCK, BLOCK)
        row_at = lax.broadcasted_iota(jnp.int32, (BLOCK, width), 0) + i * BLOCK
        lanes = lax.broadcasted_iota(jnp.int32, (BLOCK, width), 1)
        mask = jnp.where(lanes // BLOCK == i, 1.0, trans_rows[i : i + 1])
        coupling = jnp.where(row_at == lanes, 0.0, mix[rows] * mask)
        row_abs = jnp.sum(jnp.abs(coupling), axis=1, keepdims=True) + 1e-06
        retain = jnp.exp(-decay[i * BLOCK : (i + 1) * BLOCK])
        trans[rows] = jnp.where(
            row_at == lanes, retain - 1.0, (0.95 * (1.0 - retain) / row_abs) * coupling
        )


def half_kernel(flags, *refs):
    ins, (diags, high, low, turned, trans, total, keep, send, start) = refs[:2], refs[2:11]
    rows_ref, elements, quads, ahead, grams, scores, k_ref, yx_ref = refs[11:]
    width = trans.shape[0]
    chip, core = flags[0], flags[1]
    for slot in range(2):
        rows_ref[slot] = ins[slot][...]
    for j in range(4):
        rows_v = rows_ref[(chip & 1) ^ (j >> 1), (chip >> 1) ^ (j & 1)]
        scores[8 * j : 8 * j + 8] = scores_of(rows_v, turned)
        for i in range(2):
            grams[2 * j + i] = gram_of(rows_v[2 + i : 3 + i], high, low, turned)
    var = diags[0:1]
    var = (var, columns(var)[:, :1])
    t = trans[...]
    pairs = []
    for j in range(4):
        pairs.append(
            tuple(
                step_of(grams[2 * j + i], scores[8 * j + i : 8 * j + i + 1], t, var)
                for i in range(2)
            )
        )
    join(pairs, [elements.at[j] for j in range(4)], k_ref, yx_ref)
    join(
        [(parts(elements[2 * i]), parts(elements[2 * i + 1])) for i in range(2)],
        [quads.at[i] for i in range(2)],
        k_ref,
        yx_ref,
    )
    odd = chip & 1
    both = (parts(quads[0]), parts(quads[1]))
    near = core == chip >> 1
    ahead[0] = jnp.where(odd == 1, quads[0], 0.0)
    first = (parts(ahead[0]), parts(elements[2 * odd]))
    join([both, first], [total, ahead.at[1]], k_ref, yx_ref)

    @pl.when(near)
    def _():
        own = []
        for i in range(2):
            j = 2 * odd + i
            rows_v = scores[pl.ds(pl.multiple_of(8 * j, 8), 8)]
            updates = [update_of(grams[2 * j + n], rows_v[n : n + 1]) for n in range(2)]
            left = step_of(updates[0].j, rows_v[:1], trans[...], var)
            own.append((left, updates[1]))
        size = total.shape[0]
        join(own, [elements.at[i] for i in range(2)], k_ref, yx_ref)
        for i, out in ((core, keep), (1 - core, send)):
            j = 2 * odd + i
            rows_v = scores[pl.ds(pl.multiple_of(8 * j, 8), 8)]
            update = update_of(grams[2 * j], rows_v[:1])
            out[:size] = ahead[i]
            out[size : 2 * size] = elements[i]
            out[2 * size : 2 * size + width] = update.j
            out[2 * size + width :] = update.v

    lead = (core == 0) & (flags[2] == 0)

    @pl.when(lead)
    def _():
        prior = prior_of(diags[...])
        var = diags[1:2]
        left = Part(None, prior[:width], None, prior[width:], (columns(var)[:, :1], var))
        join([(left, parts(total[...]))], [state_of(start)], k_ref, yx_ref, full=False)

    @pl.when(jnp.logical_not(lead))
    def _():
        start[...] = jnp.zeros_like(start)


def pack(state, out):
    width = state.shape[1]
    half = width // 2
    rows = lax.broadcasted_iota(jnp.int32, (half, half), 0)
    lanes = lax.broadcasted_iota(jnp.int32, (half, half), 1)
    second = state[half:width, half:]
    diagonal = jnp.sum(jnp.where(rows == lanes, second, 0.0), axis=0, keepdims=True)
    out[:half, :half] = jnp.where(rows <= lanes, state[:half, :half], second)
    out[:half, half:] = state[:half, half:]
    tail = state[width:]
    at = lax.broadcasted_iota(jnp.int32, tail.shape, 0)
    diagonal = jnp.concatenate([diagonal, jnp.zeros_like(diagonal)], axis=1)
    out[half:] = jnp.where(at == 2, diagonal, tail)


def unpack(packed):
    width = packed.shape[1]
    half = width // 2
    rows = lax.broadcasted_iota(jnp.int32, (half, half), 0)
    lanes = lax.broadcasted_iota(jnp.int32, (half, half), 1)
    mixed, corner = packed[:half, :half], packed[:half, half:]
    turned = mixed.T
    first = jnp.where(rows <= lanes, mixed, turned)
    diagonal = packed[half + 2 : half + 3, :half]
    second = jnp.where(rows > lanes, mixed, jnp.where(rows < lanes, turned, diagonal))
    top = jnp.concatenate([first, corner], axis=1)
    bottom = jnp.concatenate([corner.T, second], axis=1)
    return jnp.concatenate([top, bottom]), packed[half:]


def pack_element(element, out):
    width = element.shape[1]
    rows = lax.broadcasted_iota(jnp.int32, (width, width), 0)
    lanes = lax.broadcasted_iota(jnp.int32, (width, width), 1)
    c, j = element[width : 2 * width], element[2 * width : 3 * width]
    out[:width] = element[:width]
    out[width : 2 * width] = jnp.where(rows <= lanes, c, j)
    tail = element[3 * width :]
    diagonal = jnp.sum(jnp.where(rows == lanes, j, 0.0), axis=0, keepdims=True)
    at = lax.broadcasted_iota(jnp.int32, tail.shape, 0)
    out[2 * width :] = jnp.where(at == 2, diagonal, tail)


def unpack_element(packed):
    width = packed.shape[1]
    rows = lax.broadcasted_iota(jnp.int32, (width, width), 0)
    lanes = lax.broadcasted_iota(jnp.int32, (width, width), 1)
    mixed, tail = packed[width : 2 * width], packed[2 * width :]
    turned = mixed.T
    c = jnp.where(rows <= lanes, mixed, turned)
    j = jnp.where(rows > lanes, mixed, jnp.where(rows < lanes, turned, tail[2:3]))
    return Part(packed[:width], c, j, tail)


def total_kernel(full, begins, flags, recv, own, *rest):
    *rest, k_ref, yx_ref = rest
    begin, (out, *state) = rest[:begins], rest[begins:]
    sent = (flags[1] == 0) & (full | (flags[4] == 0))

    @pl.when(sent)
    def _():
        later = flags[3] == 1
        there, here = recv[...], own[...]
        if begin:
            (start,) = begin
            width = start.shape[1]
            zero = jnp.zeros((width, width), F32)
            begun = jnp.concatenate([-eye_of(width), start[:width], zero, start[width:]])
            here = jnp.where(flags[2] == 0, begun, here)
        split = parts if begins else unpack_element
        left = split(jnp.where(later, there, here))
        right = split(jnp.where(later, here, there))
        outs = [state[0]] if full else [state_of(state[0])]
        join([(left, right)], outs, k_ref, yx_ref, full)
        (pack_element if full else pack)(state[0], out)

    @pl.when(jnp.logical_not(sent))
    def _():
        out[...] = jnp.zeros_like(out)


def block_target_kernel(flags, keep, recv, here, there, out_a, out_b, ahead, k_ref, yx_ref):
    half, core = flags[0] >> 1, flags[1]
    size, width = here.shape
    own = core == half
    pick = lambda start, end: jnp.where(own, keep[start:end], recv[start:end])
    before = jnp.where(half == 1, jnp.where(core == 0, here[...], there[...]), 0.0)
    join([(parts(before), parts(pick(0, size)))], [ahead], k_ref, yx_ref)
    left = parts(ahead[...])
    end = 2 * size + width
    first = Part(None, None, pick(2 * size, end), pick(end, keep.shape[0]))
    join(
        [(left, first), (left, parts(pick(size, 2 * size)))], [out_a, out_b], k_ref, yx_ref
    )


def target_kernel(flags, mine, other, a, b, out_a, out_b, k_ref, yx_ref):
    def after(outs, full):
        left = unpack_element(jnp.where(flags[1] == 0, mine[...], other[...]))
        join([(left, parts(a[...])), (left, parts(b[...]))], outs, k_ref, yx_ref, full)

    first = flags[5] == 1

    @pl.when((flags[3] == 1) & jnp.logical_not(first))
    def _():
        after([out_a, out_b], True)

    @pl.when((flags[3] == 1) & first)
    def _():
        width = k_ref.shape[1]
        for out in (out_a, out_b):
            out[:width] = -eye_of(width)
            out[2 * width : 3 * width] = jnp.zeros((width, width), F32)
        after([(o.at[width : 2 * width], o.at[3 * width :]) for o in (out_a, out_b)], False)

    @pl.when(flags[3] == 0)
    def _():
        out_a[...] = a[...]
        out_b[...] = b[...]


def final_kernel(flags, mine, other, diags, a, b, mean, cov, out_a, out_b, k_ref, yx_ref):
    width = k_ref.shape[1]
    early = flags[4] == 0
    done = early & (flags[2] > 0)
    outs = (out_a, out_b)

    @pl.when(jnp.logical_not(done))
    def _():
        cov_in, tail = unpack(jnp.where(flags[1] == 0, mine[...], other[...]))
        prior = prior_of(diags[...])
        cov_in = jnp.where(early, prior[:width], cov_in)
        left = Part(None, cov_in, None, jnp.where(early, prior[width:], tail))
        states = [state_of(out) for out in outs]
        join([(left, parts(a[...])), (left, parts(b[...]))], states, k_ref, yx_ref, full=False)

    @pl.when(done)
    def _():
        for target, out in zip((a, b), outs):
            out[:width] = target[width : 2 * width]
            out[width:] = target[3 * width :]

    for i, out in enumerate(outs):
        cov[i] = out[:width]
        mean[i : i + 1] = out[width : width + 1]


def shards(
    observations,
    obs_precision,
    obs_values,
    obs_pattern,
    mix_values,
    trans_pattern,
    decay_rate,
    process_var,
    prior_mean,
    prior_var,
):
    units, width = obs_values.shape
    element = (3 * width + TAIL, width)
    state = (width + TAIL, width)
    ahead = (2 * element[0] + width + TAIL, width)
    link = (2 * width + TAIL, width)
    count = lax.axis_size("outer") * lax.axis_size("inner")
    levels = int(math.log2(count))
    place = lax.axis_index("outer") * lax.axis_size("inner") + lax.axis_index("inner")
    cube = 2 * width**3
    evens = range(0, count, 2)
    across = [(i, i + 1) for i in evens]

    def flags_of(first, level=2):
        begun = ((place >> (level + 1)) == 0).astype(place.dtype)
        return jnp.stack([(place >> 1) & 3, place & 1, place >> 3, first, place >> (levels - 1), begun])

    cores = [(i, i ^ 1) for i in range(count)]
    rows = jnp.concatenate([observations, obs_precision])
    beside = lax.ppermute(rows, AXES, cores)
    pair = jnp.stack([rows, beside])
    received = []
    for turn in range(2):
        moves = []
        for i in range(count):
            chip = i % 8 // 2
            goal = 2 * (i & 1) + (turn ^ (chip & 1))
            moves.append((i, i - i % 8 + 2 * goal + (chip >> 1)))
        received.append(lax.ppermute(pair, AXES, moves))
    vectors = [v[None] for v in (process_var, prior_var, prior_mean, decay_rate)]
    patterns = jnp.concatenate([obs_pattern.T, trans_pattern.T], axis=1).astype(F32)
    patterns = jnp.pad(patterns, ((0, 0), (0, width - patterns.shape[1])))
    diags = jnp.concatenate(vectors + [patterns])
    model = call(
        prep_kernel,
        "prep",
        [((units, width), BF16), ((units, width), BF16), (width, units), (width, width)],
        [diags, obs_values, mix_values],
        0,
        width,
        4 * cube,
    )
    received, model = lax.optimization_barrier((received, model))
    flags = flags_of(place & 1)
    here, keep, send, start = call(
        half_kernel,
        "half",
        [element, ahead, ahead, state],
        [flags, *received, diags, *model],
        4,
        width,
        150 * cube,
        scalars=1,
        extra=[
            pltpu.VMEM((2, 2, 4, units), F32),
            pltpu.VMEM((4,) + element, F32),
            pltpu.VMEM((2,) + element, F32),
            pltpu.VMEM((2,) + element, F32),
            pltpu.VMEM((8, width, width), F32),
            pltpu.VMEM((32, width), F32),
        ],
        limit=36,
    )
    there = lax.ppermute(here, AXES, cores)
    send, there = lax.optimization_barrier((send, there))
    recv = lax.ppermute(send, AXES, cores)
    packed = (width // 2 + TAIL, width)
    total = here
    for level in range(2, levels - 1):
        full = level < levels - 2
        if level == 2:
            incoming = there
        else:
            incoming = mine
            flags = flags_of((place >> level) & 1, level)
        (total,) = call(
            functools.partial(total_kernel, full, int(level == 2)),
            "total",
            [link if full else packed],
            [flags, incoming, total] + ([start] if level == 2 else []),
            0,
            width,
            15 * cube,
            scalars=1,
            extra=[pltpu.VMEM(element if full else state, F32)] + scratch(1, width),
        )
        step = 2 << level
        if full:
            mine = lax.ppermute(total, AXES, [(i, i ^ step) for i in evens])
        else:
            early = [i for i in evens if i < step]
            mine = lax.ppermute(total, AXES, [(i, i ^ step) for i in early])
            other = lax.ppermute(total, AXES, [(i, (i ^ step) + 1) for i in early])
        if level > 2:
            incoming, total = lax.optimization_barrier((incoming, total))
            held = (incoming, lax.ppermute(incoming, AXES, across))
        if level == 2:
            targets = call(
                block_target_kernel,
                "block_targets",
                [element] * 2,
                [flags, keep, recv, here, there],
                0,
                width,
                45 * cube,
                scalars=1,
                extra=[pltpu.VMEM(element, F32)] + scratch(2, width),
            )
        else:
            targets = call(
                target_kernel,
                "targets",
                [element] * 2,
                [flags, *held, *targets],
                2,
                width,
                30 * cube,
                scalars=1,
            )
        mine, targets = lax.optimization_barrier((mine, targets))
    return call(
        final_kernel,
        "final",
        [(2, width), (2, width, width)],
        [flags, mine, other, diags, *targets],
        0,
        width,
        30 * cube,
        scalars=1,
        extra=[pltpu.VMEM(state, F32)] * 2 + scratch(2, width),
    )


def solution(mesh):
    split = P(AXES, None)
    in_specs = (split, split) + (P(),) * 8
    out_specs = (split, P(AXES, None, None))
    return jax.shard_map(shards, mesh=mesh, in_specs=in_specs, out_specs=out_specs, check_vma=False)
```
